32 devices in a mesh: groups: 2 (over y), seq: 4 (over z), dp: 2 (over x), sub: 2 (over core).
Axes of the slice: x: 2, y: 2, z: 4, core: 2. Of those that a mesh axis runs over, the one named last changes fastest.
Arguments:
- queries: bfloat16 [4, 512, 2048], P(('groups', 'dp'), 'seq', 'sub'), parts along dimension 0, may hold values from 0.019897461 to 1
- key_vectors: bfloat16 [4, 512, 2048], P(('groups', 'dp'), 'seq', 'sub'), parts along dimension 0, may hold values from 0.019897461 to 1
- value_vectors: bfloat16 [4, 512, 2048], P(('groups', 'dp'), 'seq', 'sub'), parts along dimension 0, may hold values from -6 to 6
- out_weight: bfloat16 [2048, 4096], P('sub', ('seq', 'dp')), may hold values from -0.125 to 0.125
- out_cotangent: bfloat16 [4, 512, 4096], P(('groups', 'dp'), 'seq'), parts along dimension 0, may hold values from -6 to 6
Outputs:
- layer_output: bfloat16 [4, 512, 4096], P(('groups', 'dp'), 'seq', 'sub'), parts along dimension 0
- query_grad: bfloat16 [4, 512, 2048], P(('groups', 'dp'), 'seq', 'sub'), parts along dimension 0
- key_grad: bfloat16 [4, 512, 2048], P(('groups', 'dp'), 'seq', 'sub'), parts along dimension 0
- value_grad: bfloat16 [4, 512, 2048], P(('groups', 'dp'), 'seq', 'sub'), parts along dimension 0
The draws below stay inside these ranges and needn't reach their ends.
There are 2 independent parts, one for each index of `groups`. The reference program is written for one: setup_inputs(seed, part) draws one part's arguments, and reference() takes and returns one part's arrays. A program takes and returns all parts, laid end to end along the dimension named above; an argument that names none is the same for every part. Nothing has to cross between parts.
All inputs are finite; a program needn't handle non-finite values.
Results may differ from the reference program's by a relative error of at most 0.009.
Values may be sent and summed in bfloat16 or wider, within the bound.
A program may use at most 128 MiB of HBM per device.

```python
import math
import jax
import jax.numpy as jnp
from jax import lax

D = 4096
HEADS = 16
HS = 128
CH = 128
SEQS = 2
LEN = 512


def steps_of(key, shape, cuts, smallest, high):
    loudness, own = 1.0, jax.random.fold_in(key, 6)
    for axis_at, shards_of in cuts:
        steps = jnp.exp(jax.random.uniform(jax.random.fold_in(own, axis_at), (shards_of,), jnp.float32, smallest / len(cuts), high / len(cuts)))
        loudness = loudness * jnp.repeat(steps, shape[axis_at] // shards_of).reshape([-1 if axis == axis_at else 1 for axis in range(len(shape))])
    return loudness


def normal_values(rng, dims, width, most, pieces=(), kind=jnp.bfloat16):
    values = jax.random.normal(rng, dims, jnp.float32) * width
    if len(pieces) > 0:
        values = steps_of(rng, dims, pieces, -0.22, 0.18) * values
    return jnp.clip(values, min=-most, max=most).astype(kind)


def setup_inputs(seed: int = 0, part: int = 0) -> dict:
    keys = jax.random.split(jax.random.key(seed), 6)
    own_keys = jax.random.split(jax.random.fold_in(keys[5], part), 6)
    queries = jnp.clip(jnp.exp(math.log(1.0) - 3.9171631 * jax.random.uniform(own_keys[0], (SEQS, LEN, HEADS * HS), jnp.float32) ** steps_of(own_keys[0], (SEQS, LEN, HEADS * HS), ((0, 2), (1, 4), (2, 2)), -0.2, 0.2)), 0.019897461, 1.0).astype(jnp.bfloat16)
    key_vectors = jnp.clip(jnp.exp(math.log(1.0) - 3.9171631 * jax.random.uniform(own_keys[1], (SEQS, LEN, HEADS * HS), jnp.float32) ** steps_of(own_keys[1], (SEQS, LEN, HEADS * HS), ((0, 2), (1, 4), (2, 2)), -0.2, 0.2)), 0.019897461, 1.0).astype(jnp.bfloat16)
    value_vectors = normal_values(own_keys[2], (SEQS, LEN, HEADS * HS), 1.0, 6.0, ((0, 2), (1, 4), (2, 2)))
    out_weight = normal_values(keys[3], (HEADS * HS, D), (HEADS * HS) ** -0.5, 0.125, ((0, 2), (1, 8)))
    out_cotangent = normal_values(own_keys[4], (SEQS, LEN, D), 1.0, 6.0, ((0, 2), (1, 4)))
    return {"queries": queries, "key_vectors": key_vectors, "value_vectors": value_vectors, "out_weight": out_weight, "out_cotangent": out_cotangent}


def rounded(tensor):
    return lax.optimization_barrier(tensor.astype(jnp.bfloat16)).astype(jnp.float32)

def rms_factor(attention):
    return lax.rsqrt(lax.optimization_barrier(jnp.mean(attention * attention, axis=-1, keepdims=True)) + 1e-05)

def reference(queries, key_vectors, value_vectors, out_weight, out_cotangent):
    sequences, length, features = queries.shape
    blocks = length // CH

    def to_heads(tensor):
        return tensor.astype(jnp.float32).reshape(sequences, blocks, CH, HEADS, HS)
    query_heads = to_heads(queries)
    key_heads = to_heads(key_vectors)
    value_heads = to_heads(value_vectors)
    positions = lax.broadcasted_iota(jnp.int32, (CH, CH), 0)
    columns = lax.broadcasted_iota(jnp.int32, (CH, CH), 1)
    causal = (columns <= positions).astype(jnp.float32)
    local_state = jnp.einsum('nbchi,nbchj->nbhij', key_heads, value_heads)
    zero_block = jnp.zeros_like(local_state[:, :1])
    prefix_state = jnp.cumsum(jnp.concatenate([zero_block, local_state[:, :-1]], axis=1), axis=1)
    prefix_rounded = rounded(prefix_state)
    block_scores = rounded(jnp.einsum('nbshi,nbthi->nbhst', query_heads, key_heads) * causal)
    attention = jnp.einsum('nbshi,nbhij->nbshj', query_heads, prefix_rounded)
    attention = attention + jnp.einsum('nbhst,nbthj->nbshj', block_scores, value_heads)
    factor = rms_factor(attention)
    normed = (attention * factor).astype(jnp.bfloat16).reshape(sequences * length, features)
    layer_output = jnp.dot(normed, out_weight, preferred_element_type=jnp.float32)
    layer_output = layer_output.astype(jnp.bfloat16).reshape(sequences, length, -1)
    cotangent = out_cotangent.reshape(sequences * length, -1)
    normed_grad = jnp.dot(cotangent, out_weight.T, preferred_element_type=jnp.float32)
    normed_grad = normed_grad.reshape(sequences, blocks, CH, HEADS, HS)
    mean_term = lax.optimization_barrier(jnp.mean(attention * normed_grad, axis=-1, keepdims=True))
    attention_grad = rounded(factor * normed_grad - attention * (factor * factor * factor) * mean_term)
    grad_scores = rounded(jnp.einsum('nbshj,nbthj->nbhst', attention_grad, value_heads) * causal)
    local_grad = jnp.einsum('nbchi,nbchj->nbhij', query_heads, attention_grad)
    shifted = jnp.concatenate([local_grad[:, 1:], zero_block], axis=1)
    suffix_state = jnp.flip(jnp.cumsum(jnp.flip(shifted, axis=1), axis=1), axis=1)
    suffix_rounded = rounded(suffix_state)
    query_grad = jnp.einsum('nbshj,nbhij->nbshi', attention_grad, prefix_rounded)
    query_grad = query_grad + jnp.einsum('nbhst,nbthi->nbshi', grad_scores, key_heads)
    key_grad = jnp.einsum('nbthj,nbhij->nbthi', value_heads, suffix_rounded)
    key_grad = key_grad + jnp.einsum('nbhst,nbshi->nbthi', grad_scores, query_heads)
    value_grad = jnp.einsum('nbthi,nbhij->nbthj', key_heads, suffix_rounded)
    value_grad = value_grad + jnp.einsum('nbhst,nbshj->nbthj', block_scores, attention_grad)

    def finish(tensor):
        return tensor.astype(jnp.bfloat16).reshape(sequences, length, features)
    return (layer_output, finish(query_grad), finish(key_grad), finish(value_grad))
```

```python
import functools

import jax
import jax.numpy as jnp
from jax import lax
from jax.experimental import pallas as pl
from jax.experimental.pallas import tpu as pltpu
from jax.sharding import PartitionSpec as P

HS = 128


def carried_in(value, axis, join, neutral):
    count, mine = (lax.axis_size(axis), lax.axis_index(axis))
    pieces = lax.all_gather(value, axis)
    total = jnp.full_like(value, 0) + jnp.asarray(neutral, value.dtype)

    def step(position, total):
        longer = join(total, pieces[position])
        return jnp.where(position < mine, longer, total)

    return lax.fori_loop(0, count - 1, step, total)


def prefix(shard, axis, join, neutral):
    count = lax.axis_size(axis)
    place = lax.axis_index(axis)
    ahead = count - 1 - place
    gathered = lax.all_gather(shard.astype(jnp.bfloat16), axis)
    state = jnp.zeros_like(shard) + jnp.asarray(neutral, shard.dtype)

    def one(step, state):
        source = count - 1 - step
        return join(state, lax.dynamic_index_in_dim(gathered, source, 0, False).astype(shard.dtype))

    return lax.fori_loop(0, ahead, one, state)


def add_states(earlier, later):
    return earlier + later


def rms_factor(attention):
    return lax.rsqrt(jnp.mean(attention * attention, axis=-1, keepdims=True) + 1e-05)


def causal_mask(positions_count):
    positions = lax.broadcasted_iota(jnp.int32, (positions_count, positions_count), 0)
    columns = lax.broadcasted_iota(jnp.int32, (positions_count, positions_count), 1)
    return (columns <= positions).astype(jnp.float32)


def local(queries, key_vectors, value_vectors, out_weight, out_cotangent):
    positions_count = queries.shape[1]
    features = queries.shape[2]
    head_count = features // HS
    query_heads = queries[0].reshape(positions_count, head_count, HS)
    key_heads = key_vectors[0].reshape(positions_count, head_count, HS)
    value_heads = value_vectors[0].reshape(positions_count, head_count, HS)
    causal = causal_mask(positions_count)
    local_state = jnp.einsum(
        "chi,chj->hij", key_heads, value_heads, preferred_element_type=jnp.float32
    )
    prefix_state = carried_in(local_state, "seq", add_states, jnp.zeros_like(local_state))
    prefix_rounded = prefix_state.astype(jnp.bfloat16)
    block_scores = jnp.einsum(
        "shi,thi->hst", query_heads, key_heads, preferred_element_type=jnp.float32
    )
    block_scores = (block_scores * causal).astype(jnp.bfloat16)
    attention = jnp.einsum(
        "shi,hij->shj", query_heads, prefix_rounded, preferred_element_type=jnp.float32
    )
    attention = attention + jnp.einsum(
        "hst,thj->shj", block_scores, value_heads, preferred_element_type=jnp.float32
    )
    factor = rms_factor(attention)
    normed = (attention * factor).astype(jnp.bfloat16).reshape(positions_count, features)
    cotangent = out_cotangent[0]
    weight_piece = lax.all_gather(out_weight, ("seq", "dp"), axis=1, tiled=True)
    product = jnp.dot(normed, weight_piece, preferred_element_type=jnp.float32)
    output_part = product
    normed_grad = lax.dot_general(
        cotangent, weight_piece, (((1,), (1,)), ((), ())), preferred_element_type=jnp.float32
    )
    output_part, normed_grad = (output_part, normed_grad)
    layer_output = lax.psum_scatter(
        output_part.astype(jnp.bfloat16), "sub", scatter_dimension=1, tiled=True
    )[None]
    grad_heads = normed_grad.reshape(positions_count, head_count, HS)
    mean_term = jnp.mean(attention * grad_heads, axis=-1, keepdims=True)
    attention_grad = (
        factor * grad_heads - attention * (factor * factor * factor) * mean_term
    ).astype(jnp.bfloat16)
    grad_scores = jnp.einsum(
        "shj,thj->hst", attention_grad, value_heads, preferred_element_type=jnp.float32
    )
    grad_scores = (grad_scores * causal).astype(jnp.bfloat16)
    local_grad = jnp.einsum(
        "chi,chj->hij", query_heads, attention_grad, preferred_element_type=jnp.float32
    )
    suffix_state = prefix(local_grad, "seq", add_states, jnp.zeros_like(local_grad))
    suffix_rounded = suffix_state.astype(jnp.bfloat16)
    query_grad = jnp.einsum(
        "shj,hij->shi", attention_grad, prefix_rounded, preferred_element_type=jnp.float32
    )
    query_grad = query_grad + jnp.einsum(
        "hst,thi->shi", grad_scores, key_heads, preferred_element_type=jnp.float32
    )
    key_grad = jnp.einsum(
        "thj,hij->thi", value_heads, suffix_rounded, preferred_element_type=jnp.float32
    )
    key_grad = key_grad + jnp.einsum(
        "hst,shi->thi", grad_scores, query_heads, preferred_element_type=jnp.float32
    )
    value_grad = jnp.einsum(
        "thi,hij->thj", key_heads, suffix_rounded, preferred_element_type=jnp.float32
    )
    value_grad = value_grad + jnp.einsum(
        "hst,shj->thj", block_scores, attention_grad, preferred_element_type=jnp.float32
    )

    def finish(tensor):
        return tensor.astype(jnp.bfloat16).reshape(1, positions_count, features)

    return (layer_output, finish(query_grad), finish(key_grad), finish(value_grad))


MESH = pl.DeviceIdType.MESH
F32, BF16 = jnp.float32, jnp.bfloat16
CHUNKS = 4


def dot(a, b, ca, cb):
    return lax.dot_general(a, b, (((ca,), (cb,)), ((), ())), preferred_element_type=F32)


def body(nz, head_count, rows, wd, *refs):
    (q, k, v, w, cot, out, qg, kg, vg, wg, cotg, lst, pin, pout, scores, att, normg, acc, ngs, ngr,
     osend, orecv, oacc, ofin, oin, ag, kloc, vloc, sin, sout,
     own_sem, wu_s, wu_r, wd_s, wd_r, c_s, c_r, p_s, p_r, x_s, x_r, n_s, n_r, g_s, g_r, o_s, o_r, f_s, f_r) = refs
    z, x = lax.axis_index("seq"), lax.axis_index("dp")
    y, s = lax.axis_index("groups"), lax.axis_index("sub")
    half, hb, feat = wd // 2, nz // 2, head_count * HS
    per = head_count // CHUNKS
    has_up, has_down = z < nz - 1, z > 0

    def place(j):
        return lax.rem(x + (j & 1), 2), lax.rem(y + (j >> 1), 2)

    def to_peer(j):
        xj, yj = place(j)
        return {"dp": xj, "groups": yj}

    def remote(src, dst, send, recv, device):
        return pltpu.make_async_remote_copy(
            src_ref=src, dst_ref=dst, send_sem=send, recv_sem=recv, device_id=device, device_id_type=MESH)

    up, down = {"seq": jnp.minimum(z + 1, nz - 1)}, {"seq": jnp.maximum(z - 1, 0)}
    other = {"sub": 1 - s}

    barrier = pltpu.get_barrier_semaphore()
    for j in (1, 2, 3):
        pl.semaphore_signal(barrier, inc=1, device_id=to_peer(j), device_id_type=MESH)
    pl.semaphore_signal(barrier, inc=1, device_id=other, device_id_type=MESH)

    @pl.when(has_up)
    def _():
        pl.semaphore_signal(barrier, inc=1, device_id=up, device_id_type=MESH)

    @pl.when(has_down)
    def _():
        pl.semaphore_signal(barrier, inc=1, device_id=down, device_id_type=MESH)
    pl.semaphore_wait(barrier, 4 + has_up.astype(jnp.int32) + has_down.astype(jnp.int32))

    mine = w.at[:, pl.ds(pl.multiple_of(y * half, 128), half)]

    def up_copy(src, block, d):
        return remote(src, wg.at[block], wu_s.at[d], wu_r.at[d], up)

    def down_copy(src, block, d):
        return remote(src, wg.at[block], wd_s.at[d], wd_r.at[d], down)

    @pl.when(has_up)
    def _():
        up_copy(mine, z, 0).start()

    @pl.when(has_down)
    def _():
        down_copy(mine, z, 0).start()
    own_w = pltpu.make_async_copy(mine, wg.at[z], own_sem.at[nz])
    own_w.start()

    def cot_piece(j, b):
        xj, yj = place(j)
        return cot.at[0, :, pl.ds(pl.multiple_of((b * 2 + xj) * wd + yj * half, 128), half)]

    def cot_own(b):
        return pltpu.make_async_copy(cot_piece(0, b), cotg.at[b, 0], own_sem.at[b])

    def cot_copy(j, b):
        return remote(cot_piece(j, b), cotg.at[b, j], c_s.at[j, b], c_r.at[j, b], to_peer(j))

    for b in range(nz):
        cot_own(b).start()
        for j in (1, 2, 3):
            cot_copy(j, b).start()

    def col(h):
        return slice(h * HS, (h + 1) * HS)

    def prefix_copy(g):
        part = pl.ds(g * per, per)
        return remote(pout.at[part], pin.at[part], p_s.at[g], p_r.at[g], up)

    def suffix_copy(g):
        part = pl.ds(g * per, per)
        return remote(sout.at[part], sin.at[part], x_s.at[g], x_r.at[g], down)

    for g in range(CHUNKS):
        for h in range(g * per, (g + 1) * per):
            lst[h] = dot(k[0, :, col(h)], v[0, :, col(h)], 0, 0)

        @pl.when(z == 0)
        def _():
            part = slice(g * per, (g + 1) * per)
            pout[part] = lst[part].astype(BF16)
            pin[part] = jnp.zeros((per, HS, HS), BF16)
            prefix_copy(g).start()

    causal = (lax.broadcasted_iota(jnp.int32, (rows, rows), 1) <= lax.broadcasted_iota(jnp.int32, (rows, rows), 0))
    for h in range(head_count):
        product = dot(q[0, :, col(h)], k[0, :, col(h)], 1, 1)
        scores[h] = jnp.where(causal, product, 0.0).astype(BF16)
    for h in range(head_count):
        att[h] = dot(scores[h], v[0, :, col(h)], 1, 0)

    def normed_copy(j):
        return remote(normg.at[0], normg.at[j], n_s.at[j], n_r.at[j], to_peer(j))

    tile = 256

    def add_block(b, first):
        left = cotg[b].reshape(4 * rows, half)

        @pl.loop(0, feat // tile)
        def _(t):
            part = pl.ds(pl.multiple_of(t * tile, tile), tile)
            new = dot(left, wg[b, part, :], 1, 1).reshape(4, rows, tile)
            if first:
                acc[:, :, part] = new
            else:
                acc[:, :, part] += new

    own_w.wait()
    for b in range(nz):
        cot_own(b).wait()
        for j in (1, 2, 3):
            cot_copy(j, b).wait_recv()

    @pl.loop(0, nz)
    def _(d):
        below, above = z - d, z + d
        from_below, from_above = (d > 0) & (below >= 0), (d > 0) & (above < nz)

        @pl.when(from_below)
        def _():
            up_copy(mine, below, d - 1).wait_recv()

            @pl.when(has_up)
            def _():
                up_copy(wg.at[below], below, d).start()

        @pl.when(from_above)
        def _():
            down_copy(mine, above, d - 1).wait_recv()

            @pl.when(has_down)
            def _():
                down_copy(wg.at[above], above, d).start()

        @pl.when(d == z)
        def _():
            @pl.when(z > 0)
            def _():
                for g in range(CHUNKS):
                    prefix_copy(g).wait_recv()

                    @pl.when(has_up)
                    def _():
                        part = slice(g * per, (g + 1) * per)
                        pout[part] = (pin[part].astype(F32) + lst[part]).astype(BF16)
                        prefix_copy(g).start()

            for h in range(head_count):
                total = att[h] + dot(q[0, :, col(h)], pin[h], 1, 0)
                att[h] = total
                factor = lax.rsqrt(jnp.mean(total * total, axis=-1, keepdims=True) + 1e-05)
                normg[0, :, col(h)] = (total * factor).astype(BF16)
            for j in (1, 2, 3):
                normed_copy(j).start()

        @pl.when(d == 0)
        def _():
            add_block(z, True)

        @pl.when(from_below)
        def _():
            add_block(below, False)

        @pl.when(from_above)
        def _():
            add_block(above, False)

    def grad_copy(j):
        return remote(ngs.at[j], ngr.at[j], g_s.at[j], g_r.at[j], to_peer(j))

    for j in (3, 1, 2):
        ngs[j] = acc[j].astype(BF16)
        grad_copy(j).start()

    for j in (1, 2, 3):
        normed_copy(j).wait_recv()
    sub_copy = remote(osend, orecv, o_s.at[0], o_r.at[0], other)

    @pl.loop(0, hb)
    def _(i):
        left = normg[...].reshape(4 * rows, feat)
        osend[i] = dot(left, wg[(1 - s) * hb + i], 1, 0).astype(BF16).reshape(4, rows, half)
    sub_copy.start()

    @pl.loop(0, hb)
    def _(i):
        left = normg[...].reshape(4 * rows, feat)
        oacc[i] = dot(left, wg[s * hb + i], 1, 0).reshape(4, rows, half)

    for j in (1, 2, 3):
        grad_copy(j).wait_recv()
    for g in range(CHUNKS):
        for h in range(g * per, (g + 1) * per):
            grad = acc[0, :, col(h)]
            for j in (1, 2, 3):
                grad = grad + ngr[j, :, col(h)].astype(F32)
            total = att[h]
            factor = lax.rsqrt(jnp.mean(total * total, axis=-1, keepdims=True) + 1e-05)
            mean_term = jnp.mean(total * grad, axis=-1, keepdims=True)
            turned = (factor * grad - total * (factor * factor * factor) * mean_term).astype(BF16)
            ag[h] = turned
            lst[h] = dot(q[0, :, col(h)], turned, 0, 0)

        @pl.when(z == nz - 1)
        def _():
            part = slice(g * per, (g + 1) * per)
            sout[part] = lst[part].astype(BF16)
            sin[part] = jnp.zeros((per, HS, HS), BF16)
            suffix_copy(g).start()

    for h in range(head_count):
        turned = ag[h]
        grad_scores = jnp.where(causal, dot(turned, v[0, :, col(h)], 1, 1), 0.0).astype(BF16)
        qg[0, :, col(h)] = (dot(turned, pin[h], 1, 1) + dot(grad_scores, k[0, :, col(h)], 1, 0)).astype(BF16)
        kloc[h] = dot(grad_scores, q[0, :, col(h)], 0, 0)
        vloc[h] = dot(scores[h], turned, 0, 0)

    @pl.when(has_up)
    def _():
        for g in range(CHUNKS):
            suffix_copy(g).wait_recv()

            @pl.when(has_down)
            def _():
                part = slice(g * per, (g + 1) * per)
                sout[part] = (sin[part].astype(F32) + lst[part]).astype(BF16)
                suffix_copy(g).start()

    def out_copy(i, j):
        return remote(ofin.at[i, j], oin.at[i, j], f_s.at[i, j], f_r.at[i, j], to_peer(j))

    sub_copy.wait_recv()
    for i in range(hb):
        ofin[i] = (oacc[i] + orecv[i].astype(F32)).astype(BF16)
        for j in (1, 2, 3):
            out_copy(i, j).start()

    for h in range(head_count):
        kg[0, :, col(h)] = (kloc[h] + dot(v[0, :, col(h)], sin[h], 1, 1)).astype(BF16)
        vg[0, :, col(h)] = (vloc[h] + dot(k[0, :, col(h)], sin[h], 1, 0)).astype(BF16)

    for i in range(hb):
        for j in range(4):
            xj, yj = place(j)
            part = pl.ds(pl.multiple_of((i * 2 + xj) * wd + yj * half, 128), half)
            if j == 0:
                out[0, :, part] = ofin[i, 0]
            else:
                out_copy(i, j).wait_recv()
                out[0, :, part] = oin[i, j]

    @pl.loop(0, nz)
    def _(d):
        @pl.when(has_up & (z - d >= 0))
        def _():
            up_copy(mine, z, d).wait_send()

        @pl.when(has_down & (z + d < nz))
        def _():
            down_copy(mine, z, d).wait_send()

    for g in range(CHUNKS):
        @pl.when(has_up)
        def _():
            prefix_copy(g).wait_send()

        @pl.when(has_down)
        def _():
            suffix_copy(g).wait_send()
    for j in (1, 2, 3):
        for b in range(nz):
            cot_copy(j, b).wait_send()
        normed_copy(j).wait_send()
        grad_copy(j).wait_send()
        for i in range(hb):
            out_copy(i, j).wait_send()
    sub_copy.wait_send()


def fused(nz, queries, key_vectors, value_vectors, out_weight, out_cotangent):
    rows, feat = queries.shape[1:]
    wd = out_weight.shape[1]
    heads, half, hb = feat // HS, wd // 2, nz // 2
    vmem, dma = pltpu.VMEM, pltpu.SemaphoreType.DMA
    states = (heads, HS, HS)
    inside = pl.BlockSpec(memory_space=pltpu.VMEM)
    outside = pl.BlockSpec(memory_space=pl.ANY)
    grads = jax.ShapeDtypeStruct((1, rows, feat), BF16)
    return tuple(pl.pallas_call(
        functools.partial(body, nz, heads, rows, wd),
        out_shape=(jax.ShapeDtypeStruct((1, rows, nz * wd), BF16), grads, grads, grads),
        in_specs=[inside, inside, inside, outside, outside],
        out_specs=(inside,) * 4,
        scratch_shapes=[
            vmem((nz, feat, half), BF16), vmem((nz, 4, rows, half), BF16),
            vmem(states, F32), vmem(states, BF16), vmem(states, BF16),
            vmem((heads, rows, rows), BF16), vmem((heads, rows, HS), F32),
            vmem((4, rows, feat), BF16), vmem((4, rows, feat), F32),
            vmem((4, rows, feat), BF16), vmem((4, rows, feat), BF16),
            vmem((hb, 4, rows, half), BF16), vmem((hb, 4, rows, half), BF16),
            vmem((hb, 4, rows, half), F32), vmem((hb, 4, rows, half), BF16), vmem((hb, 4, rows, half), BF16),
            vmem((heads, rows, HS), BF16), vmem((heads, rows, HS), F32), vmem((heads, rows, HS), F32),
            vmem(states, BF16), vmem(states, BF16),
            dma((nz + 1,)), dma((nz,)), dma((nz,)), dma((nz,)), dma((nz,)),
            dma((4, nz)), dma((4, nz)), dma((CHUNKS,)), dma((CHUNKS,)), dma((CHUNKS,)), dma((CHUNKS,)),
            dma((4,)), dma((4,)), dma((4,)), dma((4,)), dma((1,)), dma((1,)), dma((hb, 4)), dma((hb, 4)),
        ],
        compiler_params=pltpu.CompilerParams(
            collective_id=0, has_side_effects=True, vmem_limit_bytes=48 * 1024 * 1024),
    )(queries, key_vectors, value_vectors, out_weight, out_cotangent))


def solution(mesh):
    placed = (
        P(("groups", "dp"), "seq", "sub"),
        P(("groups", "dp"), "seq", "sub"),
        P(("groups", "dp"), "seq", "sub"),
        P("sub", ("seq", "dp")),
        P(("groups", "dp"), "seq", None),
    )
    shape = dict(mesh.shape)
    count = shape["seq"]

    def part(queries, key_vectors, value_vectors, out_weight, out_cotangent):
        args = (queries, key_vectors, value_vectors, out_weight, out_cotangent)
        fits = shape["groups"] == shape["dp"] == shape["sub"] == 2 and count % 2 == 0
        if fits and count <= 8 and out_weight.shape[1] % 256 == 0:
            return fused(count, *args)
        return local(*args)

    return jax.shard_map(
        part,
        mesh=mesh,
        in_specs=placed,
        out_specs=(
            P(("groups", "dp"), "seq", "sub"),
            P(("groups", "dp"), "seq", "sub"),
            P(("groups", "dp"), "seq", "sub"),
            P(("groups", "dp"), "seq", "sub"),
        ),
        check_vma=False,
    )
```

```python
import functools

import jax
import jax.numpy as jnp
from jax import lax
from jax.experimental import pallas as pl
from jax.experimental.pallas import tpu as pltpu
from jax.sharding import PartitionSpec as P

HS = 128


def carried_in(value, axis, join, neutral):
    count, mine = (lax.axis_size(axis), lax.axis_index(axis))
    pieces = lax.all_gather(value, axis)
    total = jnp.full_like(value, 0) + jnp.asarray(neutral, value.dtype)

    def step(position, total):
        longer = join(total, pieces[position])
        return jnp.where(position < mine, longer, total)

    return lax.fori_loop(0, count - 1, step, total)


def prefix(shard, axis, join, neutral):
    count = lax.axis_size(axis)
    place = lax.axis_index(axis)
    ahead = count - 1 - place
    gathered = lax.all_gather(shard.astype(jnp.bfloat16), axis)
    state = jnp.zeros_like(shard) + jnp.asarray(neutral, shard.dtype)

    def one(step, state):
        source = count - 1 - step
        return join(state, lax.dynamic_index_in_dim(gathered, source, 0, False).astype(shard.dtype))

    return lax.fori_loop(0, ahead, one, state)


def add_states(earlier, later):
    return earlier + later


def rms_factor(attention):
    return lax.rsqrt(jnp.mean(attention * attention, axis=-1, keepdims=True) + 1e-05)


def causal_mask(positions_count):
    positions = lax.broadcasted_iota(jnp.int32, (positions_count, positions_count), 0)
    columns = lax.broadcasted_iota(jnp.int32, (positions_count, positions_count), 1)
    return (columns <= positions).astype(jnp.float32)


def local(queries, key_vectors, value_vectors, out_weight, out_cotangent):
    positions_count = queries.shape[1]
    features = queries.shape[2]
    head_count = features // HS
    query_heads = queries[0].reshape(positions_count, head_count, HS)
    key_heads = key_vectors[0].reshape(positions_count, head_count, HS)
    value_heads = value_vectors[0].reshape(positions_count, head_count, HS)
    causal = causal_mask(positions_count)
    local_state = jnp.einsum(
        "chi,chj->hij", key_heads, value_heads, preferred_element_type=jnp.float32
    )
    prefix_state = carried_in(local_state, "seq", add_states, jnp.zeros_like(local_state))
    prefix_rounded = prefix_state.astype(jnp.bfloat16)
    block_scores = jnp.einsum(
        "shi,thi->hst", query_heads, key_heads, preferred_element_type=jnp.float32
    )
    block_scores = (block_scores * causal).astype(jnp.bfloat16)
    attention = jnp.einsum(
        "shi,hij->shj", query_heads, prefix_rounded, preferred_element_type=jnp.float32
    )
    attention = attention + jnp.einsum(
        "hst,thj->shj", block_scores, value_heads, preferred_element_type=jnp.float32
    )
    factor = rms_factor(attention)
    normed = (attention * factor).astype(jnp.bfloat16).reshape(positions_count, features)
    cotangent = out_cotangent[0]
    weight_piece = lax.all_gather(out_weight, ("seq", "dp"), axis=1, tiled=True)
    product = jnp.dot(normed, weight_piece, preferred_element_type=jnp.float32)
    output_part = product
    normed_grad = lax.dot_general(
        cotangent, weight_piece, (((1,), (1,)), ((), ())), preferred_element_type=jnp.float32
    )
    output_part, normed_grad = (output_part, normed_grad)
    layer_output = lax.psum_scatter(
        output_part.astype(jnp.bfloat16), "sub", scatter_dimension=1, tiled=True
    )[None]
    grad_heads = normed_grad.reshape(positions_count, head_count, HS)
    mean_term = jnp.mean(attention * grad_heads, axis=-1, keepdims=True)
    attention_grad = (
        factor * grad_heads - attention * (factor * factor * factor) * mean_term
    ).astype(jnp.bfloat16)
    grad_scores = jnp.einsum(
        "shj,thj->hst", attention_grad, value_heads, preferred_element_type=jnp.float32
    )
    grad_scores = (grad_scores * causal).astype(jnp.bfloat16)
    local_grad = jnp.einsum(
        "chi,chj->hij", query_heads, attention_grad, preferred_element_type=jnp.float32
    )
    suffix_state = prefix(local_grad, "seq", add_states, jnp.zeros_like(local_grad))
    suffix_rounded = suffix_state.astype(jnp.bfloat16)
    query_grad = jnp.einsum(
        "shj,hij->shi", attention_grad, prefix_rounded, preferred_element_type=jnp.float32
    )
    query_grad = query_grad + jnp.einsum(
        "hst,thi->shi", grad_scores, key_heads, preferred_element_type=jnp.float32
    )
    key_grad = jnp.einsum(
        "thj,hij->thi", value_heads, suffix_rounded, preferred_element_type=jnp.float32
    )
    key_grad = key_grad + jnp.einsum(
        "hst,shi->thi", grad_scores, query_heads, preferred_element_type=jnp.float32
    )
    value_grad = jnp.einsum(
        "thi,hij->thj", key_heads, suffix_rounded, preferred_element_type=jnp.float32
    )
    value_grad = value_grad + jnp.einsum(
        "hst,shj->thj", block_scores, attention_grad, preferred_element_type=jnp.float32
    )

    def finish(tensor):
        return tensor.astype(jnp.bfloat16).reshape(1, positions_count, features)

    return (layer_output, finish(query_grad), finish(key_grad), finish(value_grad))


MESH = pl.DeviceIdType.MESH
F32, BF16 = jnp.float32, jnp.bfloat16
CHUNKS = 4


def dot(a, b, ca, cb):
    return lax.dot_general(a, b, (((ca,), (cb,)), ((), ())), preferred_element_type=F32)


def body(nz, head_count, rows, wd, *refs):
    (q_in, k_in, v_in, w, cot, out, qg, kg, vg, wg, cotg, lst, pin, pout, scores, att, normg, acc, ngs, ngr,
     osend, orecv, oacc, ofin, oin, ag, kloc, vloc, sin, sout,
     q, k, v, in_sem, own_sem, wu_s, wu_r, wd_s, wd_r, c_s, c_r, p_s, p_r, x_s, x_r, n_s, n_r, g_s, g_r, o_s, o_r, f_s, f_r) = refs
    z, x = lax.axis_index("seq"), lax.axis_index("dp")
    y, s = lax.axis_index("groups"), lax.axis_index("sub")
    half, hb, feat = wd // 2, nz // 2, head_count * HS
    per = head_count // CHUNKS
    has_up, has_down = z < nz - 1, z > 0

    def place(j):
        return lax.rem(x + (j & 1), 2), lax.rem(y + (j >> 1), 2)

    def to_peer(j):
        xj, yj = place(j)
        return {"dp": xj, "groups": yj}

    def remote(src, dst, send, recv, device):
        return pltpu.make_async_remote_copy(
            src_ref=src, dst_ref=dst, send_sem=send, recv_sem=recv, device_id=device, device_id_type=MESH)

    up, down = {"seq": jnp.minimum(z + 1, nz - 1)}, {"seq": jnp.maximum(z - 1, 0)}
    other = {"sub": 1 - s}

    loads = [pltpu.make_async_copy(a, b, in_sem.at[i]) for i, (a, b) in enumerate(((k_in, k), (v_in, v), (q_in, q)))]
    for load in loads:
        load.start()

    barrier = pltpu.get_barrier_semaphore()
    for j in (1, 2, 3):
        pl.semaphore_signal(barrier, inc=1, device_id=to_peer(j), device_id_type=MESH)
    pl.semaphore_signal(barrier, inc=1, device_id=other, device_id_type=MESH)

    @pl.when(has_up)
    def _():
        pl.semaphore_signal(barrier, inc=1, device_id=up, device_id_type=MESH)

    @pl.when(has_down)
    def _():
        pl.semaphore_signal(barrier, inc=1, device_id=down, device_id_type=MESH)
    pl.semaphore_wait(barrier, 4 + has_up.astype(jnp.int32) + has_down.astype(jnp.int32))

    mine = w.at[:, pl.ds(pl.multiple_of(y * half, 128), half)]
    deep = feat // CHUNKS

    def source(block, d, c):
        held = mine if d == 0 else wg.at[block]
        return held.at[c * deep:(c + 1) * deep]

    def up_copy(block, d, c):
        return remote(source(block, d, c), wg.at[block, c * deep:(c + 1) * deep], wu_s.at[d, c], wu_r.at[d, c], up)

    def down_copy(block, d, c):
        return remote(source(block, d, c), wg.at[block, c * deep:(c + 1) * deep], wd_s.at[d, c], wd_r.at[d, c], down)

    def start_own(c):
        @pl.when(has_up)
        def _():
            up_copy(z, 0, c).start()

        @pl.when((z < nz - 1) & has_down)
        def _():
            down_copy(z, 0, c).start()

    start_own(0)

    @pl.when(z == nz - 1)
    def _():
        for c in range(CHUNKS):
            down_copy(z, 0, c).start()
    own_w = pltpu.make_async_copy(mine, wg.at[z], own_sem.at[nz])
    own_w.start()

    def cot_piece(j, b):
        xj, yj = place(j)
        return cot.at[0, :, pl.ds(pl.multiple_of((b * 2 + xj) * wd + yj * half, 128), half)]

    def cot_own(b):
        return pltpu.make_async_copy(cot_piece(0, b), cotg.at[b, 0], own_sem.at[b])

    def cot_copy(j, b):
        return remote(cot_piece(j, b), cotg.at[b, j], c_s.at[j, b], c_r.at[j, b], to_peer(j))

    for b in range(nz):
        cot_own(b).start()
        for j in (1, 2, 3):
            cot_copy(j, b).start()

    def col(h):
        return slice(h * HS, (h + 1) * HS)

    def prefix_copy(g):
        part = pl.ds(g * per, per)
        return remote(pout.at[part], pin.at[part], p_s.at[g], p_r.at[g], up)

    def suffix_copy(g):
        part = pl.ds(g * per, per)
        return remote(sout.at[part], sin.at[part], x_s.at[g], x_r.at[g], down)

    for load in loads:
        load.wait()
    for g in range(CHUNKS):
        for h in range(g * per, (g + 1) * per):
            lst[h] = dot(k[0, :, col(h)], v[0, :, col(h)], 0, 0)

        @pl.when(z == 0)
        def _():
            part = slice(g * per, (g + 1) * per)
            pout[part] = lst[part].astype(BF16)
            pin[part] = jnp.zeros((per, HS, HS), BF16)
            prefix_copy(g).start()

    causal = (lax.broadcasted_iota(jnp.int32, (rows, rows), 1) <= lax.broadcasted_iota(jnp.int32, (rows, rows), 0))
    for h in range(head_count):
        product = dot(q[0, :, col(h)], k[0, :, col(h)], 1, 1)
        scores[h] = jnp.where(causal, product, 0.0).astype(BF16)
    for h in range(head_count):
        att[h] = dot(scores[h], v[0, :, col(h)], 1, 0)

    def normed_copy(j):
        return remote(normg.at[0], normg.at[j], n_s.at[j], n_r.at[j], to_peer(j))

    def grad_copy(j, c):
        part = slice(c * deep, (c + 1) * deep)
        return remote(ngs.at[j, :, part], ngr.at[j, :, part], g_s.at[j, c], g_r.at[j, c], to_peer(j))

    def attend():
        @pl.when(z > 0)
        def _():
            for g in range(CHUNKS):
                prefix_copy(g).wait_recv()

                @pl.when(has_up)
                def _():
                    part = slice(g * per, (g + 1) * per)
                    pout[part] = (pin[part].astype(F32) + lst[part]).astype(BF16)
                    prefix_copy(g).start()

        for h in range(head_count):
            total = att[h] + dot(q[0, :, col(h)], pin[h], 1, 0)
            att[h] = total
            factor = lax.rsqrt(jnp.mean(total * total, axis=-1, keepdims=True) + 1e-05)
            normg[0, :, col(h)] = (total * factor).astype(BF16)
        for j in (1, 2, 3):
            normed_copy(j).start()

    def turn(g):
        for j in (1, 2, 3):
            grad_copy(j, g).wait_recv()
        for h in range(g * per, (g + 1) * per):
            grad = acc[:, col(h)]
            for j in (1, 2, 3):
                grad = grad + ngr[j, :, col(h)].astype(F32)
            total = att[h]
            factor = lax.rsqrt(jnp.mean(total * total, axis=-1, keepdims=True) + 1e-05)
            mean_term = jnp.mean(total * grad, axis=-1, keepdims=True)
            turned = (factor * grad - total * (factor * factor * factor) * mean_term).astype(BF16)
            ag[h] = turned
            lst[h] = dot(q[0, :, col(h)], turned, 0, 0)

        @pl.when(z == nz - 1)
        def _():
            part = slice(g * per, (g + 1) * per)
            sout[part] = lst[part].astype(BF16)
            sin[part] = jnp.zeros((per, HS, HS), BF16)
            suffix_copy(g).start()

    for c in range(CHUNKS):
        if c + 1 < CHUNKS:
            start_own(c + 1)
        for d in range(1, nz):
            @pl.when(z - d >= 0)
            def _():
                up_copy(z - d, d - 1, c).wait_recv()

                @pl.when(has_up)
                def _():
                    up_copy(z - d, d, c).start()

            @pl.when(z + d < nz)
            def _():
                down_copy(z + d, d - 1, c).wait_recv()

                @pl.when(has_down)
                def _():
                    down_copy(z + d, d, c).start()
        if c == 0:
            own_w.wait()
            for b in range(nz):
                cot_own(b).wait()
                for j in (1, 2, 3):
                    cot_copy(j, b).wait_recv()
        part = slice(c * deep, (c + 1) * deep)
        total = dot(cotg[0].reshape(4 * rows, half), wg[0, part, :], 1, 1)
        for b in range(1, nz):
            total = total + dot(cotg[b].reshape(4 * rows, half), wg[b, part, :], 1, 1)
        acc[:, part] = total[:rows]
        for j in (1, 2, 3):
            ngs[j, :, part] = total[j * rows:(j + 1) * rows].astype(BF16)
            grad_copy(j, c).start()
        if c == 0:
            @pl.when(z <= 1)
            def _():
                attend()
        elif c < CHUNKS - 1:
            @pl.when(z == c + 1)
            def _():
                attend()
        if c == CHUNKS - 2:
            turn(0)
        if c == CHUNKS - 1:
            for g in range(1, CHUNKS):
                turn(g)

    for j in (1, 2, 3):
        normed_copy(j).wait_recv()
    sub_copy = remote(osend, orecv, o_s.at[0], o_r.at[0], other)

    @pl.loop(0, hb)
    def _(i):
        left = normg[...].reshape(4 * rows, feat)
        osend[i] = dot(left, wg[(1 - s) * hb + i], 1, 0).astype(BF16).reshape(4, rows, half)
    sub_copy.start()

    @pl.loop(0, hb)
    def _(i):
        left = normg[...].reshape(4 * rows, feat)
        oacc[i] = dot(left, wg[s * hb + i], 1, 0).reshape(4, rows, half)

    for h in range(head_count):
        turned = ag[h]
        grad_scores = jnp.where(causal, dot(turned, v[0, :, col(h)], 1, 1), 0.0).astype(BF16)
        qg[0, :, col(h)] = (dot(turned, pin[h], 1, 1) + dot(grad_scores, k[0, :, col(h)], 1, 0)).astype(BF16)
        kloc[h] = dot(grad_scores, q[0, :, col(h)], 0, 0)
        vloc[h] = dot(scores[h], turned, 0, 0)

    @pl.when(has_up)
    def _():
        for g in range(CHUNKS):
            suffix_copy(g).wait_recv()

            @pl.when(has_down)
            def _():
                part = slice(g * per, (g + 1) * per)
                sout[part] = (sin[part].astype(F32) + lst[part]).astype(BF16)
                suffix_copy(g).start()

    def out_copy(i, j):
        return remote(ofin.at[i, j], oin.at[i, j], f_s.at[i, j], f_r.at[i, j], to_peer(j))

    sub_copy.wait_recv()
    for i in range(hb):
        ofin[i] = (oacc[i] + orecv[i].astype(F32)).astype(BF16)
        for j in (1, 2, 3):
            out_copy(i, j).start()

    for h in range(head_count):
        kg[0, :, col(h)] = (kloc[h] + dot(v[0, :, col(h)], sin[h], 1, 1)).astype(BF16)
        vg[0, :, col(h)] = (vloc[h] + dot(k[0, :, col(h)], sin[h], 1, 0)).astype(BF16)

    for i in range(hb):
        for j in range(4):
            xj, yj = place(j)
            part = pl.ds(pl.multiple_of((i * 2 + xj) * wd + yj * half, 128), half)
            if j == 0:
                out[0, :, part] = ofin[i, 0]
            else:
                out_copy(i, j).wait_recv()
                out[0, :, part] = oin[i, j]

    for c in range(CHUNKS):
        for d in range(nz - 1):
            @pl.when(has_up & (z - d >= 0))
            def _():
                up_copy(z, d, c).wait_send()

            @pl.when(has_down & (z + d < nz))
            def _():
                down_copy(z, d, c).wait_send()

    for g in range(CHUNKS):
        @pl.when(has_up)
        def _():
            prefix_copy(g).wait_send()

        @pl.when(has_down)
        def _():
            suffix_copy(g).wait_send()
    for j in (1, 2, 3):
        for b in range(nz):
            cot_copy(j, b).wait_send()
        normed_copy(j).wait_send()
        for c in range(CHUNKS):
            grad_copy(j, c).wait_send()
        for i in range(hb):
            out_copy(i, j).wait_send()
    sub_copy.wait_send()


def fused(nz, queries, key_vectors, value_vectors, out_weight, out_cotangent):
    rows, feat = queries.shape[1:]
    wd = out_weight.shape[1]
    heads, half, hb = feat // HS, wd // 2, nz // 2
    vmem, dma = pltpu.VMEM, pltpu.SemaphoreType.DMA
    states = (heads, HS, HS)
    inside = pl.BlockSpec(memory_space=pltpu.VMEM)
    outside = pl.BlockSpec(memory_space=pltpu.HBM)
    grads = jax.ShapeDtypeStruct((1, rows, feat), BF16)
    return tuple(pl.pallas_call(
        functools.partial(body, nz, heads, rows, wd),
        out_shape=(jax.ShapeDtypeStruct((1, rows, nz * wd), BF16), grads, grads, grads),
        in_specs=[outside] * 5,
        out_specs=(inside,) * 4,
        scratch_shapes=[
            vmem((nz, feat, half), BF16), vmem((nz, 4, rows, half), BF16),
            vmem(states, F32), vmem(states, BF16), vmem(states, BF16),
            vmem((heads, rows, rows), BF16), vmem((heads, rows, HS), F32),
            vmem((4, rows, feat), BF16), vmem((rows, feat), F32),
            vmem((4, rows, feat), BF16), vmem((4, rows, feat), BF16),
            vmem((hb, 4, rows, half), BF16), vmem((hb, 4, rows, half), BF16),
            vmem((hb, 4, rows, half), F32), vmem((hb, 4, rows, half), BF16), vmem((hb, 4, rows, half), BF16),
            vmem((heads, rows, HS), BF16), vmem((heads, rows, HS), F32), vmem((heads, rows, HS), F32),
            vmem(states, BF16), vmem(states, BF16),
            vmem((1, rows, feat), BF16), vmem((1, rows, feat), BF16), vmem((1, rows, feat), BF16), dma((3,)),
            dma((nz + 1,)), dma((nz, CHUNKS)), dma((nz, CHUNKS)), dma((nz, CHUNKS)), dma((nz, CHUNKS)),
            dma((4, nz)), dma((4, nz)), dma((CHUNKS,)), dma((CHUNKS,)), dma((CHUNKS,)), dma((CHUNKS,)),
            dma((4,)), dma((4,)), dma((4, CHUNKS)), dma((4, CHUNKS)), dma((1,)), dma((1,)), dma((hb, 4)), dma((hb, 4)),
        ],
        compiler_params=pltpu.CompilerParams(
            collective_id=0, has_side_effects=True, vmem_limit_bytes=60 * 1024 * 1024),
    )(queries, key_vectors, value_vectors, out_weight, out_cotangent))


def solution(mesh):
    placed = (
        P(("groups", "dp"), "seq", "sub"),
        P(("groups", "dp"), "seq", "sub"),
        P(("groups", "dp"), "seq", "sub"),
        P("sub", ("seq", "dp")),
        P(("groups", "dp"), "seq", None),
    )
    shape = dict(mesh.shape)
    count = shape["seq"]

    def part(queries, key_vectors, value_vectors, out_weight, out_cotangent):
        args = (queries, key_vectors, value_vectors, out_weight, out_cotangent)
        fits = shape["groups"] == shape["dp"] == shape["sub"] == 2 and count % 2 == 0
        if fits and count <= 4 and out_weight.shape[1] % 256 == 0:
            return fused(count, *args)
        return local(*args)

    return jax.shard_map(
        part,
        mesh=mesh,
        in_specs=placed,
        out_specs=(
            P(("groups", "dp"), "seq", "sub"),
            P(("groups", "dp"), "seq", "sub"),
            P(("groups", "dp"), "seq", "sub"),
            P(("groups", "dp"), "seq", "sub"),
        ),
        check_vma=False,
    )
```

```python
import functools

import jax
import jax.numpy as jnp
from jax import lax
from jax.experimental import pallas as pl
from jax.experimental.pallas import tpu as pltpu
from jax.sharding import PartitionSpec as P

HS = 128


def carried_in(value, axis, join, neutral):
    count, mine = (lax.axis_size(axis), lax.axis_index(axis))
    pieces = lax.all_gather(value, axis)
    total = jnp.full_like(value, 0) + jnp.asarray(neutral, value.dtype)

    def step(position, total):
        longer = join(total, pieces[position])
        return jnp.where(position < mine, longer, total)

    return lax.fori_loop(0, count - 1, step, total)


def prefix(shard, axis, join, neutral):
    count = lax.axis_size(axis)
    place = lax.axis_index(axis)
    ahead = count - 1 - place
    gathered = lax.all_gather(shard.astype(jnp.bfloat16), axis)
    state = jnp.zeros_like(shard) + jnp.asarray(neutral, shard.dtype)

    def one(step, state):
        source = count - 1 - step
        return join(state, lax.dynamic_index_in_dim(gathered, source, 0, False).astype(shard.dtype))

    return lax.fori_loop(0, ahead, one, state)


def add_states(earlier, later):
    return earlier + later


def rms_factor(attention):
    return lax.rsqrt(jnp.mean(attention * attention, axis=-1, keepdims=True) + 1e-05)


def causal_mask(positions_count):
    positions = lax.broadcasted_iota(jnp.int32, (positions_count, positions_count), 0)
    columns = lax.broadcasted_iota(jnp.int32, (positions_count, positions_count), 1)
    return (columns <= positions).astype(jnp.float32)


def local(queries, key_vectors, value_vectors, out_weight, out_cotangent):
    positions_count = queries.shape[1]
    features = queries.shape[2]
    head_count = features // HS
    query_heads = queries[0].reshape(positions_count, head_count, HS)
    key_heads = key_vectors[0].reshape(positions_count, head_count, HS)
    value_heads = value_vectors[0].reshape(positions_count, head_count, HS)
    causal = causal_mask(positions_count)
    local_state = jnp.einsum(
        "chi,chj->hij", key_heads, value_heads, preferred_element_type=jnp.float32
    )
    prefix_state = carried_in(local_state, "seq", add_states, jnp.zeros_like(local_state))
    prefix_rounded = prefix_state.astype(jnp.bfloat16)
    block_scores = jnp.einsum(
        "shi,thi->hst", query_heads, key_heads, preferred_element_type=jnp.float32
    )
    block_scores = (block_scores * causal).astype(jnp.bfloat16)
    attention = jnp.einsum(
        "shi,hij->shj", query_heads, prefix_rounded, preferred_element_type=jnp.float32
    )
    attention = attention + jnp.einsum(
        "hst,thj->shj", block_scores, value_heads, preferred_element_type=jnp.float32
    )
    factor = rms_factor(attention)
    normed = (attention * factor).astype(jnp.bfloat16).reshape(positions_count, features)
    cotangent = out_cotangent[0]
    weight_piece = lax.all_gather(out_weight, ("seq", "dp"), axis=1, tiled=True)
    product = jnp.dot(normed, weight_piece, preferred_element_type=jnp.float32)
    output_part = product
    normed_grad = lax.dot_general(
        cotangent, weight_piece, (((1,), (1,)), ((), ())), preferred_element_type=jnp.float32
    )
    output_part, normed_grad = (output_part, normed_grad)
    layer_output = lax.psum_scatter(
        output_part.astype(jnp.bfloat16), "sub", scatter_dimension=1, tiled=True
    )[None]
    grad_heads = normed_grad.reshape(positions_count, head_count, HS)
    mean_term = jnp.mean(attention * grad_heads, axis=-1, keepdims=True)
    attention_grad = (
        factor * grad_heads - attention * (factor * factor * factor) * mean_term
    ).astype(jnp.bfloat16)
    grad_scores = jnp.einsum(
        "shj,thj->hst", attention_grad, value_heads, preferred_element_type=jnp.float32
    )
    grad_scores = (grad_scores * causal).astype(jnp.bfloat16)
    local_grad = jnp.einsum(
        "chi,chj->hij", query_heads, attention_grad, preferred_element_type=jnp.float32
    )
    suffix_state = prefix(local_grad, "seq", add_states, jnp.zeros_like(local_grad))
    suffix_rounded = suffix_state.astype(jnp.bfloat16)
    query_grad = jnp.einsum(
        "shj,hij->shi", attention_grad, prefix_rounded, preferred_element_type=jnp.float32
    )
    query_grad = query_grad + jnp.einsum(
        "hst,thi->shi", grad_scores, key_heads, preferred_element_type=jnp.float32
    )
    key_grad = jnp.einsum(
        "thj,hij->thi", value_heads, suffix_rounded, preferred_element_type=jnp.float32
    )
    key_grad = key_grad + jnp.einsum(
        "hst,shi->thi", grad_scores, query_heads, preferred_element_type=jnp.float32
    )
    value_grad = jnp.einsum(
        "thi,hij->thj", key_heads, suffix_rounded, preferred_element_type=jnp.float32
    )
    value_grad = value_grad + jnp.einsum(
        "hst,shj->thj", block_scores, attention_grad, preferred_element_type=jnp.float32
    )

    def finish(tensor):
        return tensor.astype(jnp.bfloat16).reshape(1, positions_count, features)

    return (layer_output, finish(query_grad), finish(key_grad), finish(value_grad))


MESH = pl.DeviceIdType.MESH
F32, BF16 = jnp.float32, jnp.bfloat16
CHUNKS = 4


def dot(a, b, ca, cb):
    return lax.dot_general(a, b, (((ca,), (cb,)), ((), ())), preferred_element_type=F32)


def body(nz, head_count, rows, wd, *refs):
    (q_in, k_in, v_in, w, cot, out, qg, kg, vg, wg, cotg, lst, pin, pout, scores, att, normg, acc, ngs, ngr,
     osend, orecv, oacc, ofin, oin, ag, kloc, vloc, sin, sout,
     q, k, v, in_sem, own_sem, wu_s, wu_r, wd_s, wd_r, c_s, c_r, p_s, p_r, x_s, x_r, n_s, n_r, g_s, g_r, o_s, o_r, f_s, f_r) = refs
    z, x = lax.axis_index("seq"), lax.axis_index("dp")
    y, s = lax.axis_index("groups"), lax.axis_index("sub")
    half, hb, feat = wd // 2, nz // 2, head_count * HS
    per = head_count // CHUNKS
    has_up, has_down = z < nz - 1, z > 0

    def place(j):
        return lax.rem(x + (j & 1), 2), lax.rem(y + (j >> 1), 2)

    def to_peer(j):
        xj, yj = place(j)
        return {"dp": xj, "groups": yj}

    def remote(src, dst, send, recv, device):
        return pltpu.make_async_remote_copy(
            src_ref=src, dst_ref=dst, send_sem=send, recv_sem=recv, device_id=device, device_id_type=MESH)

    up, down = {"seq": jnp.minimum(z + 1, nz - 1)}, {"seq": jnp.maximum(z - 1, 0)}
    other = {"sub": 1 - s}

    loads = [pltpu.make_async_copy(a, b, in_sem.at[i]) for i, (a, b) in enumerate(((k_in, k), (v_in, v), (q_in, q)))]
    for load in loads:
        load.start()

    barrier = pltpu.get_barrier_semaphore()
    for j in (1, 2, 3):
        pl.semaphore_signal(barrier, inc=1, device_id=to_peer(j), device_id_type=MESH)
    pl.semaphore_signal(barrier, inc=1, device_id=other, device_id_type=MESH)

    @pl.when(has_up)
    def _():
        pl.semaphore_signal(barrier, inc=1, device_id=up, device_id_type=MESH)

    @pl.when(has_down)
    def _():
        pl.semaphore_signal(barrier, inc=1, device_id=down, device_id_type=MESH)
    partners = 4 + has_up.astype(jnp.int32) + has_down.astype(jnp.int32)
    for far in (2, -2):
        near = (z + far < nz) if far > 0 else (z + far >= 0)
        partners += near.astype(jnp.int32)

        @pl.when(near)
        def _():
            pl.semaphore_signal(
                barrier, inc=1, device_id={"seq": jnp.clip(z + far, 0, nz - 1)}, device_id_type=MESH)
    pl.semaphore_wait(barrier, partners)

    mine = w.at[:, pl.ds(pl.multiple_of(y * half, 128), half)]
    deep = feat // CHUNKS

    def chunk(ref, c):
        return ref.at[c * deep:(c + 1) * deep]

    def far_copy(far, c):
        block = wg.at[z]
        i = 1 if far > 0 else 0
        target = {"seq": jnp.clip(z + far, 0, nz - 1)}
        return remote(chunk(mine, c), chunk(block, c), wu_s.at[abs(far) - 1, i, c], wu_r.at[abs(far) - 1, i, c], target)

    def pass_copy(step, c):
        block = wg.at[jnp.clip(z - 2 * step, 0, nz - 1)]
        i = 1 if step > 0 else 0
        return remote(chunk(block, c), chunk(block, c), wd_s.at[i, c], wd_r.at[i, c], up if step > 0 else down)

    def within(far):
        return (z + far < nz) if far > 0 else (z + far >= 0)

    def start_own(c):
        for far in (2, -2, 1, -1):
            if abs(far) < nz:
                @pl.when(within(far))
                def _():
                    far_copy(far, c).start()

    start_own(0)
    start_own(1)
    own_w = pltpu.make_async_copy(mine, wg.at[z], own_sem.at[nz])
    own_w.start()

    def cot_piece(j, b):
        xj, yj = place(j)
        return cot.at[0, :, pl.ds(pl.multiple_of((b * 2 + xj) * wd + yj * half, 128), half)]

    def cot_own(b):
        return pltpu.make_async_copy(cot_piece(0, b), cotg.at[b, 0], own_sem.at[b])

    def cot_copy(j, b):
        return remote(cot_piece(j, b), cotg.at[b, j], c_s.at[j, b], c_r.at[j, b], to_peer(j))

    for b in range(nz):
        cot_own(b).start()
        for j in (1, 2, 3):
            cot_copy(j, b).start()

    def col(h):
        return slice(h * HS, (h + 1) * HS)

    def prefix_copy(g):
        part = pl.ds(g * per, per)
        return remote(pout.at[part], pin.at[part], p_s.at[g], p_r.at[g], up)

    def suffix_copy(g):
        part = pl.ds(g * per, per)
        return remote(sout.at[part], sin.at[part], x_s.at[g], x_r.at[g], down)

    for load in loads:
        load.wait()
    for g in range(CHUNKS):
        for h in range(g * per, (g + 1) * per):
            lst[h] = dot(k[0, :, col(h)], v[0, :, col(h)], 0, 0)

        @pl.when(z == 0)
        def _():
            part = slice(g * per, (g + 1) * per)
            pout[part] = lst[part].astype(BF16)
            pin[part] = jnp.zeros((per, HS, HS), BF16)
            prefix_copy(g).start()

    causal = (lax.broadcasted_iota(jnp.int32, (rows, rows), 1) <= lax.broadcasted_iota(jnp.int32, (rows, rows), 0))
    for h in range(head_count):
        product = dot(q[0, :, col(h)], k[0, :, col(h)], 1, 1)
        scores[h] = jnp.where(causal, product, 0.0).astype(BF16)
    for h in range(head_count):
        att[h] = dot(scores[h], v[0, :, col(h)], 1, 0)

    def normed_copy(j):
        return remote(normg.at[0], normg.at[j], n_s.at[j], n_r.at[j], to_peer(j))

    def grad_copy(j, c):
        part = slice(c * deep, (c + 1) * deep)
        return remote(ngs.at[j, :, part], ngr.at[j, :, part], g_s.at[j, c], g_r.at[j, c], to_peer(j))

    def attend():
        @pl.when(z > 0)
        def _():
            for g in range(CHUNKS):
                prefix_copy(g).wait_recv()

                @pl.when(has_up)
                def _():
                    part = slice(g * per, (g + 1) * per)
                    pout[part] = (pin[part].astype(F32) + lst[part]).astype(BF16)
                    prefix_copy(g).start()

        for h in range(head_count):
            total = att[h] + dot(q[0, :, col(h)], pin[h], 1, 0)
            att[h] = total
            factor = lax.rsqrt(jnp.mean(total * total, axis=-1, keepdims=True) + 1e-05)
            normg[0, :, col(h)] = (total * factor).astype(BF16)
        for j in (1, 2, 3):
            normed_copy(j).start()

    def turn(g):
        for j in (1, 2, 3):
            grad_copy(j, g).wait_recv()
        for h in range(g * per, (g + 1) * per):
            grad = acc[:, col(h)]
            for j in (1, 2, 3):
                grad = grad + ngr[j, :, col(h)].astype(F32)
            total = att[h]
            factor = lax.rsqrt(jnp.mean(total * total, axis=-1, keepdims=True) + 1e-05)
            mean_term = jnp.mean(total * grad, axis=-1, keepdims=True)
            turned = (factor * grad - total * (factor * factor * factor) * mean_term).astype(BF16)
            ag[h] = turned
            lst[h] = dot(q[0, :, col(h)], turned, 0, 0)

        @pl.when(z == nz - 1)
        def _():
            part = slice(g * per, (g + 1) * per)
            sout[part] = lst[part].astype(BF16)
            sin[part] = jnp.zeros((per, HS, HS), BF16)
            suffix_copy(g).start()

    for c in range(CHUNKS):
        if c + 2 < CHUNKS:
            start_own(c + 2)
        if nz > 2:
            for step in (1, -1):
                @pl.when(within(-2 * step))
                def _():
                    far_copy(2 * step, c).wait_recv()

                if nz > 3:
                    @pl.when(within(-2 * step) & within(step))
                    def _():
                        pass_copy(step, c).start()
        for step in (1, -1):
            @pl.when(within(-step))
            def _():
                far_copy(step, c).wait_recv()

            if nz > 3:
                @pl.when(within(-3 * step))
                def _():
                    pass_copy(step, c).wait_recv()
        if c == 0:
            own_w.wait()
            for b in range(nz):
                cot_own(b).wait()
                for j in (1, 2, 3):
                    cot_copy(j, b).wait_recv()
        part = slice(c * deep, (c + 1) * deep)
        total = dot(cotg[0].reshape(4 * rows, half), wg[0, part, :], 1, 1)
        for b in range(1, nz):
            total = total + dot(cotg[b].reshape(4 * rows, half), wg[b, part, :], 1, 1)
        acc[:, part] = total[:rows]
        for j in (1, 2, 3):
            ngs[j, :, part] = total[j * rows:(j + 1) * rows].astype(BF16)
            grad_copy(j, c).start()
        if c == 0:
            @pl.when(z <= 1)
            def _():
                attend()
        elif c < CHUNKS - 1:
            @pl.when(z == c + 1)
            def _():
                attend()
        if c == CHUNKS - 2:
            turn(0)
        if c == CHUNKS - 1:
            for g in range(1, CHUNKS):
                turn(g)

    for j in (1, 2, 3):
        normed_copy(j).wait_recv()
    sub_copy = remote(osend, orecv, o_s.at[0], o_r.at[0], other)

    @pl.loop(0, hb)
    def _(i):
        left = normg[...].reshape(4 * rows, feat)
        osend[i] = dot(left, wg[(1 - s) * hb + i], 1, 0).astype(BF16).reshape(4, rows, half)
    sub_copy.start()

    def hop():
        for g in range(CHUNKS):
            suffix_copy(g).wait_recv()

            @pl.when(has_down)
            def _():
                part = slice(g * per, (g + 1) * per)
                sout[part] = (sin[part].astype(F32) + lst[part]).astype(BF16)
                suffix_copy(g).start()

    @pl.when(z == nz - 2)
    def _():
        hop()

    @pl.loop(0, hb)
    def _(i):
        left = normg[...].reshape(4 * rows, feat)
        oacc[i] = dot(left, wg[s * hb + i], 1, 0).reshape(4, rows, half)

    for h in range(head_count):
        turned = ag[h]
        grad_scores = jnp.where(causal, dot(turned, v[0, :, col(h)], 1, 1), 0.0).astype(BF16)
        qg[0, :, col(h)] = (dot(turned, pin[h], 1, 1) + dot(grad_scores, k[0, :, col(h)], 1, 0)).astype(BF16)
        kloc[h] = dot(grad_scores, q[0, :, col(h)], 0, 0)
        vloc[h] = dot(scores[h], turned, 0, 0)

    def out_copy(i, j):
        return remote(ofin.at[i, j], oin.at[i, j], f_s.at[i, j], f_r.at[i, j], to_peer(j))

    sub_copy.wait_recv()
    for i in range(hb):
        ofin[i] = (oacc[i] + orecv[i].astype(F32)).astype(BF16)
        for j in (1, 2, 3):
            out_copy(i, j).start()

    @pl.when(z < nz - 2)
    def _():
        hop()

    for h in range(head_count):
        kg[0, :, col(h)] = (kloc[h] + dot(v[0, :, col(h)], sin[h], 1, 1)).astype(BF16)
        vg[0, :, col(h)] = (vloc[h] + dot(k[0, :, col(h)], sin[h], 1, 0)).astype(BF16)

    for i in range(hb):
        for j in range(4):
            xj, yj = place(j)
            part = pl.ds(pl.multiple_of((i * 2 + xj) * wd + yj * half, 128), half)
            if j == 0:
                out[0, :, part] = ofin[i, 0]
            else:
                out_copy(i, j).wait_recv()
                out[0, :, part] = oin[i, j]

    for c in range(CHUNKS):
        for far in (2, -2, 1, -1):
            if abs(far) < nz:
                @pl.when(within(far))
                def _():
                    far_copy(far, c).wait_send()

        if nz > 3:
            for step in (1, -1):
                @pl.when(within(-2 * step) & within(step))
                def _():
                    pass_copy(step, c).wait_send()

    for g in range(CHUNKS):
        @pl.when(has_up)
        def _():
            prefix_copy(g).wait_send()

        @pl.when(has_down)
        def _():
            suffix_copy(g).wait_send()
    for j in (1, 2, 3):
        for b in range(nz):
            cot_copy(j, b).wait_send()
        normed_copy(j).wait_send()
        for c in range(CHUNKS):
            grad_copy(j, c).wait_send()
        for i in range(hb):
            out_copy(i, j).wait_send()
    sub_copy.wait_send()


def fused(nz, queries, key_vectors, value_vectors, out_weight, out_cotangent):
    rows, feat = queries.shape[1:]
    wd = out_weight.shape[1]
    heads, half, hb = feat // HS, wd // 2, nz // 2
    vmem, dma = pltpu.VMEM, pltpu.SemaphoreType.DMA
    states = (heads, HS, HS)
    inside = pl.BlockSpec(memory_space=pltpu.VMEM)
    outside = pl.BlockSpec(memory_space=pltpu.HBM)
    grads = jax.ShapeDtypeStruct((1, rows, feat), BF16)
    return tuple(pl.pallas_call(
        functools.partial(body, nz, heads, rows, wd),
        out_shape=(jax.ShapeDtypeStruct((1, rows, nz * wd), BF16), grads, grads, grads),
        in_specs=[outside] * 5,
        out_specs=(inside,) * 4,
        scratch_shapes=[
            vmem((nz, feat, half), BF16), vmem((nz, 4, rows, half), BF16),
            vmem(states, F32), vmem(states, BF16), vmem(states, BF16),
            vmem((heads, rows, rows), BF16), vmem((heads, rows, HS), F32),
            vmem((4, rows, feat), BF16), vmem((rows, feat), F32),
            vmem((4, rows, feat), BF16), vmem((4, rows, feat), BF16),
            vmem((hb, 4, rows, half), BF16), vmem((hb, 4, rows, half), BF16),
            vmem((hb, 4, rows, half), F32), vmem((hb, 4, rows, half), BF16), vmem((hb, 4, rows, half), BF16),
            vmem((heads, rows, HS), BF16), vmem((heads, rows, HS), F32), vmem((heads, rows, HS), F32),
            vmem(states, BF16), vmem(states, BF16),
            vmem((1, rows, feat), BF16), vmem((1, rows, feat), BF16), vmem((1, rows, feat), BF16), dma((3,)),
            dma((nz + 1,)), dma((2, 2, CHUNKS)), dma((2, 2, CHUNKS)), dma((2, CHUNKS)), dma((2, CHUNKS)),
            dma((4, nz)), dma((4, nz)), dma((CHUNKS,)), dma((CHUNKS,)), dma((CHUNKS,)), dma((CHUNKS,)),
            dma((4,)), dma((4,)), dma((4, CHUNKS)), dma((4, CHUNKS)), dma((1,)), dma((1,)), dma((hb, 4)), dma((hb, 4)),
        ],
        compiler_params=pltpu.CompilerParams(
            collective_id=0, has_side_effects=True, vmem_limit_bytes=55 * 1024 * 1024),
    )(queries, key_vectors, value_vectors, out_weight, out_cotangent))


def solution(mesh):
    placed = (
        P(("groups", "dp"), "seq", "sub"),
        P(("groups", "dp"), "seq", "sub"),
        P(("groups", "dp"), "seq", "sub"),
        P("sub", ("seq", "dp")),
        P(("groups", "dp"), "seq", None),
    )
    shape = dict(mesh.shape)
    count = shape["seq"]

    def part(queries, key_vectors, value_vectors, out_weight, out_cotangent):
        args = (queries, key_vectors, value_vectors, out_weight, out_cotangent)
        fits = shape["groups"] == shape["dp"] == shape["sub"] == 2 and count % 2 == 0
        if fits and count <= 4 and out_weight.shape[1] % 256 == 0:
            return fused(count, *args)
        return local(*args)

    return jax.shard_map(
        part,
        mesh=mesh,
        in_specs=placed,
        out_specs=(
            P(("groups", "dp"), "seq", "sub"),
            P(("groups", "dp"), "seq", "sub"),
            P(("groups", "dp"), "seq", "sub"),
            P(("groups", "dp"), "seq", "sub"),
        ),
        check_vma=False,
    )
```

```python
import functools

import jax
import jax.numpy as jnp
from jax import lax
from jax.experimental import pallas as pl
from jax.experimental.pallas import tpu as pltpu
from jax.sharding import PartitionSpec as P

HS = 128


def carried_in(value, axis, join, neutral):
    count, mine = (lax.axis_size(axis), lax.axis_index(axis))
    pieces = lax.all_gather(value, axis)
    total = jnp.full_like(value, 0) + jnp.asarray(neutral, value.dtype)

    def step(position, total):
        longer = join(total, pieces[position])
        return jnp.where(position < mine, longer, total)

    return lax.fori_loop(0, count - 1, step, total)


def prefix(shard, axis, join, neutral):
    count = lax.axis_size(axis)
    place = lax.axis_index(axis)
    ahead = count - 1 - place
    gathered = lax.all_gather(shard.astype(jnp.bfloat16), axis)
    state = jnp.zeros_like(shard) + jnp.asarray(neutral, shard.dtype)

    def one(step, state):
        source = count - 1 - step
        return join(state, lax.dynamic_index_in_dim(gathered, source, 0, False).astype(shard.dtype))

    return lax.fori_loop(0, ahead, one, state)


def add_states(earlier, later):
    return earlier + later


def rms_factor(attention):
    return lax.rsqrt(jnp.mean(attention * attention, axis=-1, keepdims=True) + 1e-05)


def causal_mask(positions_count):
    positions = lax.broadcasted_iota(jnp.int32, (positions_count, positions_count), 0)
    columns = lax.broadcasted_iota(jnp.int32, (positions_count, positions_count), 1)
    return (columns <= positions).astype(jnp.float32)


def local(queries, key_vectors, value_vectors, out_weight, out_cotangent):
    positions_count = queries.shape[1]
    features = queries.shape[2]
    head_count = features // HS
    query_heads = queries[0].reshape(positions_count, head_count, HS)
    key_heads = key_vectors[0].reshape(positions_count, head_count, HS)
    value_heads = value_vectors[0].reshape(positions_count, head_count, HS)
    causal = causal_mask(positions_count)
    local_state = jnp.einsum(
        "chi,chj->hij", key_heads, value_heads, preferred_element_type=jnp.float32
    )
    prefix_state = carried_in(local_state, "seq", add_states, jnp.zeros_like(local_state))
    prefix_rounded = prefix_state.astype(jnp.bfloat16)
    block_scores = jnp.einsum(
        "shi,thi->hst", query_heads, key_heads, preferred_element_type=jnp.float32
    )
    block_scores = (block_scores * causal).astype(jnp.bfloat16)
    attention = jnp.einsum(
        "shi,hij->shj", query_heads, prefix_rounded, preferred_element_type=jnp.float32
    )
    attention = attention + jnp.einsum(
        "hst,thj->shj", block_scores, value_heads, preferred_element_type=jnp.float32
    )
    factor = rms_factor(attention)
    normed = (attention * factor).astype(jnp.bfloat16).reshape(positions_count, features)
    cotangent = out_cotangent[0]
    weight_piece = lax.all_gather(out_weight, ("seq", "dp"), axis=1, tiled=True)
    product = jnp.dot(normed, weight_piece, preferred_element_type=jnp.float32)
    output_part = product
    normed_grad = lax.dot_general(
        cotangent, weight_piece, (((1,), (1,)), ((), ())), preferred_element_type=jnp.float32
    )
    output_part, normed_grad = (output_part, normed_grad)
    layer_output = lax.psum_scatter(
        output_part.astype(jnp.bfloat16), "sub", scatter_dimension=1, tiled=True
    )[None]
    grad_heads = normed_grad.reshape(positions_count, head_count, HS)
    mean_term = jnp.mean(attention * grad_heads, axis=-1, keepdims=True)
    attention_grad = (
        factor * grad_heads - attention * (factor * factor * factor) * mean_term
    ).astype(jnp.bfloat16)
    grad_scores = jnp.einsum(
        "shj,thj->hst", attention_grad, value_heads, preferred_element_type=jnp.float32
    )
    grad_scores = (grad_scores * causal).astype(jnp.bfloat16)
    local_grad = jnp.einsum(
        "chi,chj->hij", query_heads, attention_grad, preferred_element_type=jnp.float32
    )
    suffix_state = prefix(local_grad, "seq", add_states, jnp.zeros_like(local_grad))
    suffix_rounded = suffix_state.astype(jnp.bfloat16)
    query_grad = jnp.einsum(
        "shj,hij->shi", attention_grad, prefix_rounded, preferred_element_type=jnp.float32
    )
    query_grad = query_grad + jnp.einsum(
        "hst,thi->shi", grad_scores, key_heads, preferred_element_type=jnp.float32
    )
    key_grad = jnp.einsum(
        "thj,hij->thi", value_heads, suffix_rounded, preferred_element_type=jnp.float32
    )
    key_grad = key_grad + jnp.einsum(
        "hst,shi->thi", grad_scores, query_heads, preferred_element_type=jnp.float32
    )
    value_grad = jnp.einsum(
        "thi,hij->thj", key_heads, suffix_rounded, preferred_element_type=jnp.float32
    )
    value_grad = value_grad + jnp.einsum(
        "hst,shj->thj", block_scores, attention_grad, preferred_element_type=jnp.float32
    )

    def finish(tensor):
        return tensor.astype(jnp.bfloat16).reshape(1, positions_count, features)

    return (layer_output, finish(query_grad), finish(key_grad), finish(value_grad))


MESH = pl.DeviceIdType.MESH
F32, BF16 = jnp.float32, jnp.bfloat16
CHUNKS = 4


def dot(a, b, ca, cb):
    return lax.dot_general(a, b, (((ca,), (cb,)), ((), ())), preferred_element_type=F32)


def body(nz, head_count, rows, wd, *refs):
    (q_in, k_in, v_in, w, cot, out, qg, kg, vg, wg, cotg, lst, pin, pout, scores, att, normg, acc, ngs, ngr,
     osend, orecv, oacc, ofin, oin, ag, kloc, vloc, sin, sout,
     q, k, v, in_sem, own_sem, wu_s, wu_r, wd_s, wd_r, c_s, c_r, p_s, p_r, x_s, x_r, n_s, n_r, g_s, g_r, o_s, o_r, f_s, f_r) = refs
    z, x = lax.axis_index("seq"), lax.axis_index("dp")
    y, s = lax.axis_index("groups"), lax.axis_index("sub")
    half, hb, feat = wd // 2, nz // 2, head_count * HS
    per = head_count // CHUNKS
    has_up, has_down = z < nz - 1, z > 0

    def place(j):
        return lax.rem(x + (j & 1), 2), lax.rem(y + (j >> 1), 2)

    def to_peer(j):
        xj, yj = place(j)
        return {"dp": xj, "groups": yj}

    def remote(src, dst, send, recv, device):
        return pltpu.make_async_remote_copy(
            src_ref=src, dst_ref=dst, send_sem=send, recv_sem=recv, device_id=device, device_id_type=MESH)

    up, down = {"seq": jnp.minimum(z + 1, nz - 1)}, {"seq": jnp.maximum(z - 1, 0)}
    other = {"sub": 1 - s}

    loads = [pltpu.make_async_copy(a, b, in_sem.at[i]) for i, (a, b) in enumerate(((k_in, k), (v_in, v), (q_in, q)))]
    for load in loads:
        load.start()

    barrier = pltpu.get_barrier_semaphore()
    for j in (1, 2, 3):
        pl.semaphore_signal(barrier, inc=1, device_id=to_peer(j), device_id_type=MESH)
    pl.semaphore_signal(barrier, inc=1, device_id=other, device_id_type=MESH)

    @pl.when(has_up)
    def _():
        pl.semaphore_signal(barrier, inc=1, device_id=up, device_id_type=MESH)

    @pl.when(has_down)
    def _():
        pl.semaphore_signal(barrier, inc=1, device_id=down, device_id_type=MESH)
    pl.semaphore_wait(barrier, 4 + has_up.astype(jnp.int32) + has_down.astype(jnp.int32))

    mine = w.at[:, pl.ds(pl.multiple_of(y * half, 128), half)]
    deep = feat // CHUNKS

    def source(block, d, c):
        held = mine if d == 0 else wg.at[block]
        return held.at[c * deep:(c + 1) * deep]

    def up_copy(block, d, c):
        return remote(source(block, d, c), wg.at[block, c * deep:(c + 1) * deep], wu_s.at[d, c], wu_r.at[d, c], up)

    def down_copy(block, d, c):
        return remote(source(block, d, c), wg.at[block, c * deep:(c + 1) * deep], wd_s.at[d, c], wd_r.at[d, c], down)

    def start_own(c):
        @pl.when(has_up)
        def _():
            up_copy(z, 0, c).start()

        @pl.when((z < nz - 1) & has_down)
        def _():
            down_copy(z, 0, c).start()

    start_own(0)

    @pl.when(z == nz - 1)
    def _():
        for c in range(CHUNKS):
            down_copy(z, 0, c).start()
    own_w = pltpu.make_async_copy(mine, wg.at[z], own_sem.at[nz])
    own_w.start()

    def cot_piece(j, b):
        xj, yj = place(j)
        return cot.at[0, :, pl.ds(pl.multiple_of((b * 2 + xj) * wd + yj * half, 128), half)]

    def cot_own(b):
        return pltpu.make_async_copy(cot_piece(0, b), cotg.at[b, 0], own_sem.at[b])

    def cot_copy(j, b):
        return remote(cot_piece(j, b), cotg.at[b, j], c_s.at[j, b], c_r.at[j, b], to_peer(j))

    for b in range(nz):
        cot_own(b).start()
        for j in (1, 2, 3):
            cot_copy(j, b).start()

    def col(h):
        return slice(h * HS, (h + 1) * HS)

    def prefix_copy(g):
        part = pl.ds(g * per, per)
        return remote(pout.at[part], pin.at[part], p_s.at[g], p_r.at[g], up)

    def suffix_copy(g):
        part = pl.ds(g * per, per)
        return remote(sout.at[part], sin.at[part], x_s.at[g], x_r.at[g], down)

    for load in loads:
        load.wait()
    for g in range(CHUNKS):
        for h in range(g * per, (g + 1) * per):
            lst[h] = dot(k[0, :, col(h)], v[0, :, col(h)], 0, 0)

        @pl.when(z == 0)
        def _():
            part = slice(g * per, (g + 1) * per)
            pout[part] = lst[part].astype(BF16)
            pin[part] = jnp.zeros((per, HS, HS), BF16)
            prefix_copy(g).start()

    causal = (lax.broadcasted_iota(jnp.int32, (rows, rows), 1) <= lax.broadcasted_iota(jnp.int32, (rows, rows), 0))
    for h in range(head_count):
        product = dot(q[0, :, col(h)], k[0, :, col(h)], 1, 1)
        scores[h] = jnp.where(causal, product, 0.0).astype(BF16)
    for h in range(head_count):
        att[h] = dot(scores[h], v[0, :, col(h)], 1, 0)

    def normed_copy(j):
        return remote(normg.at[0], normg.at[j], n_s.at[j], n_r.at[j], to_peer(j))

    def grad_copy(j, c):
        part = slice(c * deep, (c + 1) * deep)
        return remote(ngs.at[j, :, part], ngr.at[j, :, part], g_s.at[j, c], g_r.at[j, c], to_peer(j))

    def attend():
        @pl.when(z > 0)
        def _():
            for g in range(CHUNKS):
                prefix_copy(g).wait_recv()

                @pl.when(has_up)
                def _():
                    part = slice(g * per, (g + 1) * per)
                    pout[part] = (pin[part].astype(F32) + lst[part]).astype(BF16)
                    prefix_copy(g).start()

        for h in range(head_count):
            total = att[h] + dot(q[0, :, col(h)], pin[h], 1, 0)
            att[h] = total
            factor = lax.rsqrt(jnp.mean(total * total, axis=-1, keepdims=True) + 1e-05)
            normg[0, :, col(h)] = (total * factor).astype(BF16)
        for j in (1, 2, 3):
            normed_copy(j).start()

    def turn(g):
        for j in (1, 2, 3):
            grad_copy(j, g).wait_recv()
        for h in range(g * per, (g + 1) * per):
            grad = acc[:, col(h)]
            for j in (1, 2, 3):
                grad = grad + ngr[j, :, col(h)].astype(F32)
            total = att[h]
            factor = lax.rsqrt(jnp.mean(total * total, axis=-1, keepdims=True) + 1e-05)
            mean_term = jnp.mean(total * grad, axis=-1, keepdims=True)
            turned = (factor * grad - total * (factor * factor * factor) * mean_term).astype(BF16)
            ag[h] = turned
            lst[h] = dot(q[0, :, col(h)], turned, 0, 0)

        @pl.when(z == nz - 1)
        def _():
            part = slice(g * per, (g + 1) * per)
            sout[part] = lst[part].astype(BF16)
            sin[part] = jnp.zeros((per, HS, HS), BF16)
            suffix_copy(g).start()

    for c in range(CHUNKS):
        if c + 1 < CHUNKS:
            start_own(c + 1)
        for d in range(1, nz):
            @pl.when(z - d >= 0)
            def _():
                up_copy(z - d, d - 1, c).wait_recv()

                @pl.when(has_up)
                def _():
                    up_copy(z - d, d, c).start()

            @pl.when(z + d < nz)
            def _():
                down_copy(z + d, d - 1, c).wait_recv()

                @pl.when(has_down)
                def _():
                    down_copy(z + d, d, c).start()
        if c == 0:
            own_w.wait()
            for b in range(nz):
                cot_own(b).wait()
                for j in (1, 2, 3):
                    cot_copy(j, b).wait_recv()
        part = slice(c * deep, (c + 1) * deep)
        total = dot(cotg[0].reshape(4 * rows, half), wg[0, part, :], 1, 1)
        for b in range(1, nz):
            total = total + dot(cotg[b].reshape(4 * rows, half), wg[b, part, :], 1, 1)
        acc[:, part] = total[:rows]
        for j in (1, 2, 3):
            ngs[j, :, part] = total[j * rows:(j + 1) * rows].astype(BF16)
            grad_copy(j, c).start()
        if c == 0:
            @pl.when(z <= 1)
            def _():
                attend()
        elif c < CHUNKS - 1:
            @pl.when(z == c + 1)
            def _():
                attend()
        if c == CHUNKS - 2:
            turn(0)
        if c == CHUNKS - 1:
            for g in range(1, CHUNKS - 1):
                turn(g)

    for j in (1, 2, 3):
        normed_copy(j).wait_recv()
    sub_copy = remote(osend, orecv, o_s.at[0], o_r.at[0], other)

    @pl.loop(0, hb)
    def _(i):
        left = normg[...].reshape(4 * rows, feat)
        osend[i] = dot(left, wg[(1 - s) * hb + i], 1, 0).astype(BF16).reshape(4, rows, half)
    sub_copy.start()

    @pl.loop(0, hb)
    def _(i):
        left = normg[...].reshape(4 * rows, feat)
        oacc[i] = dot(left, wg[s * hb + i], 1, 0).reshape(4, rows, half)

    turn(CHUNKS - 1)

    def out_copy(i, j):
        return remote(ofin.at[i, j], oin.at[i, j], f_s.at[i, j], f_r.at[i, j], to_peer(j))

    sub_copy.wait_recv()
    for i in range(hb):
        ofin[i] = (oacc[i] + orecv[i].astype(F32)).astype(BF16)
        for j in (1, 2, 3):
            out_copy(i, j).start()

    for h in range(head_count):
        turned = ag[h]
        grad_scores = jnp.where(causal, dot(turned, v[0, :, col(h)], 1, 1), 0.0).astype(BF16)
        qg[0, :, col(h)] = (dot(turned, pin[h], 1, 1) + dot(grad_scores, k[0, :, col(h)], 1, 0)).astype(BF16)
        kloc[h] = dot(grad_scores, q[0, :, col(h)], 0, 0)
        vloc[h] = dot(scores[h], turned, 0, 0)

    @pl.when(has_up)
    def _():
        for g in range(CHUNKS):
            suffix_copy(g).wait_recv()

            @pl.when(has_down)
            def _():
                part = slice(g * per, (g + 1) * per)
                sout[part] = (sin[part].astype(F32) + lst[part]).astype(BF16)
                suffix_copy(g).start()

    for h in range(head_count):
        kg[0, :, col(h)] = (kloc[h] + dot(v[0, :, col(h)], sin[h], 1, 1)).astype(BF16)
        vg[0, :, col(h)] = (vloc[h] + dot(k[0, :, col(h)], sin[h], 1, 0)).astype(BF16)

    for i in range(hb):
        for j in range(4):
            xj, yj = place(j)
            part = pl.ds(pl.multiple_of((i * 2 + xj) * wd + yj * half, 128), half)
            if j == 0:
                out[0, :, part] = ofin[i, 0]
            else:
                out_copy(i, j).wait_recv()
                out[0, :, part] = oin[i, j]

    for c in range(CHUNKS):
        for d in range(nz - 1):
            @pl.when(has_up & (z - d >= 0))
            def _():
                up_copy(z, d, c).wait_send()

            @pl.when(has_down & (z + d < nz))
            def _():
                down_copy(z, d, c).wait_send()

    for g in range(CHUNKS):
        @pl.when(has_up)
        def _():
            prefix_copy(g).wait_send()

        @pl.when(has_down)
        def _():
            suffix_copy(g).wait_send()
    for j in (1, 2, 3):
        for b in range(nz):
            cot_copy(j, b).wait_send()
        normed_copy(j).wait_send()
        for c in range(CHUNKS):
            grad_copy(j, c).wait_send()
        for i in range(hb):
            out_copy(i, j).wait_send()
    sub_copy.wait_send()


def fused(nz, queries, key_vectors, value_vectors, out_weight, out_cotangent):
    rows, feat = queries.shape[1:]
    wd = out_weight.shape[1]
    heads, half, hb = feat // HS, wd // 2, nz // 2
    vmem, dma = pltpu.VMEM, pltpu.SemaphoreType.DMA
    states = (heads, HS, HS)
    inside = pl.BlockSpec(memory_space=pltpu.VMEM)
    outside = pl.BlockSpec(memory_space=pltpu.HBM)
    grads = jax.ShapeDtypeStruct((1, rows, feat), BF16)
    return tuple(pl.pallas_call(
        functools.partial(body, nz, heads, rows, wd),
        out_shape=(jax.ShapeDtypeStruct((1, rows, nz * wd), BF16), grads, grads, grads),
        in_specs=[outside] * 5,
        out_specs=(inside,) * 4,
        scratch_shapes=[
            vmem((nz, feat, half), BF16), vmem((nz, 4, rows, half), BF16),
            vmem(states, F32), vmem(states, BF16), vmem(states, BF16),
            vmem((heads, rows, rows), BF16), vmem((heads, rows, HS), F32),
            vmem((4, rows, feat), BF16), vmem((rows, feat), F32),
            vmem((4, rows, feat), BF16), vmem((4, rows, feat), BF16),
            vmem((hb, 4, rows, half), BF16), vmem((hb, 4, rows, half), BF16),
            vmem((hb, 4, rows, half), F32), vmem((hb, 4, rows, half), BF16), vmem((hb, 4, rows, half), BF16),
            vmem((heads, rows, HS), BF16), vmem((heads, rows, HS), F32), vmem((heads, rows, HS), F32),
            vmem(states, BF16), vmem(states, BF16),
            vmem((1, rows, feat), BF16), vmem((1, rows, feat), BF16), vmem((1, rows, feat), BF16), dma((3,)),
            dma((nz + 1,)), dma((nz, CHUNKS)), dma((nz, CHUNKS)), dma((nz, CHUNKS)), dma((nz, CHUNKS)),
            dma((4, nz)), dma((4, nz)), dma((CHUNKS,)), dma((CHUNKS,)), dma((CHUNKS,)), dma((CHUNKS,)),
            dma((4,)), dma((4,)), dma((4, CHUNKS)), dma((4, CHUNKS)), dma((1,)), dma((1,)), dma((hb, 4)), dma((hb, 4)),
        ],
        compiler_params=pltpu.CompilerParams(
            collective_id=0, has_side_effects=True, vmem_limit_bytes=60 * 1024 * 1024),
    )(queries, key_vectors, value_vectors, out_weight, out_cotangent))


def solution(mesh):
    placed = (
        P(("groups", "dp"), "seq", "sub"),
        P(("groups", "dp"), "seq", "sub"),
        P(("groups", "dp"), "seq", "sub"),
        P("sub", ("seq", "dp")),
        P(("groups", "dp"), "seq", None),
    )
    shape = dict(mesh.shape)
    count = shape["seq"]

    def part(queries, key_vectors, value_vectors, out_weight, out_cotangent):
        args = (queries, key_vectors, value_vectors, out_weight, out_cotangent)
        fits = shape["groups"] == shape["dp"] == shape["sub"] == 2 and count % 2 == 0
        if fits and count <= 4 and out_weight.shape[1] % 256 == 0:
            return fused(count, *args)
        return local(*args)

    return jax.shard_map(
        part,
        mesh=mesh,
        in_specs=placed,
        out_specs=(
            P(("groups", "dp"), "seq", "sub"),
            P(("groups", "dp"), "seq", "sub"),
            P(("groups", "dp"), "seq", "sub"),
            P(("groups", "dp"), "seq", "sub"),
        ),
        check_vma=False,
    )
```

```python
import functools

import jax
import jax.numpy as jnp
from jax import lax
from jax.experimental import pallas as pl
from jax.experimental.pallas import tpu as pltpu
from jax.sharding import PartitionSpec as P

HS = 128


def carried_in(value, axis, join, neutral):
    count, mine = (lax.axis_size(axis), lax.axis_index(axis))
    pieces = lax.all_gather(value, axis)
    total = jnp.full_like(value, 0) + jnp.asarray(neutral, value.dtype)

    def step(position, total):
        longer = join(total, pieces[position])
        return jnp.where(position < mine, longer, total)

    return lax.fori_loop(0, count - 1, step, total)


def prefix(shard, axis, join, neutral):
    count = lax.axis_size(axis)
    place = lax.axis_index(axis)
    ahead = count - 1 - place
    gathered = lax.all_gather(shard.astype(jnp.bfloat16), axis)
    state = jnp.zeros_like(shard) + jnp.asarray(neutral, shard.dtype)

    def one(step, state):
        source = count - 1 - step
        return join(state, lax.dynamic_index_in_dim(gathered, source, 0, False).astype(shard.dtype))

    return lax.fori_loop(0, ahead, one, state)


def add_states(earlier, later):
    return earlier + later


def rms_factor(attention):
    return lax.rsqrt(jnp.mean(attention * attention, axis=-1, keepdims=True) + 1e-05)


def causal_mask(positions_count):
    positions = lax.broadcasted_iota(jnp.int32, (positions_count, positions_count), 0)
    columns = lax.broadcasted_iota(jnp.int32, (positions_count, positions_count), 1)
    return (columns <= positions).astype(jnp.float32)


def local(queries, key_vectors, value_vectors, out_weight, out_cotangent):
    positions_count = queries.shape[1]
    features = queries.shape[2]
    head_count = features // HS
    query_heads = queries[0].reshape(positions_count, head_count, HS)
    key_heads = key_vectors[0].reshape(positions_count, head_count, HS)
    value_heads = value_vectors[0].reshape(positions_count, head_count, HS)
    causal = causal_mask(positions_count)
    local_state = jnp.einsum(
        "chi,chj->hij", key_heads, value_heads, preferred_element_type=jnp.float32
    )
    prefix_state = carried_in(local_state, "seq", add_states, jnp.zeros_like(local_state))
    prefix_rounded = prefix_state.astype(jnp.bfloat16)
    block_scores = jnp.einsum(
        "shi,thi->hst", query_heads, key_heads, preferred_element_type=jnp.float32
    )
    block_scores = (block_scores * causal).astype(jnp.bfloat16)
    attention = jnp.einsum(
        "shi,hij->shj", query_heads, prefix_rounded, preferred_element_type=jnp.float32
    )
    attention = attention + jnp.einsum(
        "hst,thj->shj", block_scores, value_heads, preferred_element_type=jnp.float32
    )
    factor = rms_factor(attention)
    normed = (attention * factor).astype(jnp.bfloat16).reshape(positions_count, features)
    cotangent = out_cotangent[0]
    weight_piece = lax.all_gather(out_weight, ("seq", "dp"), axis=1, tiled=True)
    product = jnp.dot(normed, weight_piece, preferred_element_type=jnp.float32)
    output_part = product
    normed_grad = lax.dot_general(
        cotangent, weight_piece, (((1,), (1,)), ((), ())), preferred_element_type=jnp.float32
    )
    output_part, normed_grad = (output_part, normed_grad)
    layer_output = lax.psum_scatter(
        output_part.astype(jnp.bfloat16), "sub", scatter_dimension=1, tiled=True
    )[None]
    grad_heads = normed_grad.reshape(positions_count, head_count, HS)
    mean_term = jnp.mean(attention * grad_heads, axis=-1, keepdims=True)
    attention_grad = (
        factor * grad_heads - attention * (factor * factor * factor) * mean_term
    ).astype(jnp.bfloat16)
    grad_scores = jnp.einsum(
        "shj,thj->hst", attention_grad, value_heads, preferred_element_type=jnp.float32
    )
    grad_scores = (grad_scores * causal).astype(jnp.bfloat16)
    local_grad = jnp.einsum(
        "chi,chj->hij", query_heads, attention_grad, preferred_element_type=jnp.float32
    )
    suffix_state = prefix(local_grad, "seq", add_states, jnp.zeros_like(local_grad))
    suffix_rounded = suffix_state.astype(jnp.bfloat16)
    query_grad = jnp.einsum(
        "shj,hij->shi", attention_grad, prefix_rounded, preferred_element_type=jnp.float32
    )
    query_grad = query_grad + jnp.einsum(
        "hst,thi->shi", grad_scores, key_heads, preferred_element_type=jnp.float32
    )
    key_grad = jnp.einsum(
        "thj,hij->thi", value_heads, suffix_rounded, preferred_element_type=jnp.float32
    )
    key_grad = key_grad + jnp.einsum(
        "hst,shi->thi", grad_scores, query_heads, preferred_element_type=jnp.float32
    )
    value_grad = jnp.einsum(
        "thi,hij->thj", key_heads, suffix_rounded, preferred_element_type=jnp.float32
    )
    value_grad = value_grad + jnp.einsum(
        "hst,shj->thj", block_scores, attention_grad, preferred_element_type=jnp.float32
    )

    def finish(tensor):
        return tensor.astype(jnp.bfloat16).reshape(1, positions_count, features)

    return (layer_output, finish(query_grad), finish(key_grad), finish(value_grad))


MESH = pl.DeviceIdType.MESH
F32, BF16 = jnp.float32, jnp.bfloat16
CHUNKS = 4


def dot(a, b, ca, cb):
    return lax.dot_general(a, b, (((ca,), (cb,)), ((), ())), preferred_element_type=F32)


def body(nz, head_count, rows, wd, *refs):
    (q_in, k_in, v_in, w, cot, out, qg, kg, vg, wg, cotg, lst, pin, pout, scores, att, normg, acc, ngs, ngr,
     osend, orecv, oacc, ofin, oin, ag, kloc, vloc, sin, sout,
     q, k, v, in_sem, own_sem, wu_s, wu_r, wd_s, wd_r, c_s, c_r, p_s, p_r, x_s, x_r, n_s, n_r, g_s, g_r, o_s, o_r, f_s, f_r) = refs
    z, x = lax.axis_index("seq"), lax.axis_index("dp")
    y, s = lax.axis_index("groups"), lax.axis_index("sub")
    half, hb, feat = wd // 2, nz // 2, head_count * HS
    per = head_count // CHUNKS
    has_up, has_down = z < nz - 1, z > 0

    def place(j):
        return lax.rem(x + (j & 1), 2), lax.rem(y + (j >> 1), 2)

    def to_peer(j):
        xj, yj = place(j)
        return {"dp": xj, "groups": yj}

    def remote(src, dst, send, recv, device):
        return pltpu.make_async_remote_copy(
            src_ref=src, dst_ref=dst, send_sem=send, recv_sem=recv, device_id=device, device_id_type=MESH)

    up, down = {"seq": jnp.minimum(z + 1, nz - 1)}, {"seq": jnp.maximum(z - 1, 0)}
    other = {"sub": 1 - s}

    loads = [pltpu.make_async_copy(a, b, in_sem.at[i]) for i, (a, b) in enumerate(((k_in, k), (v_in, v), (q_in, q)))]
    for load in loads:
        load.start()

    barrier = pltpu.get_barrier_semaphore()
    for j in (1, 2, 3):
        pl.semaphore_signal(barrier, inc=1, device_id=to_peer(j), device_id_type=MESH)
    pl.semaphore_signal(barrier, inc=1, device_id=other, device_id_type=MESH)

    @pl.when(has_up)
    def _():
        pl.semaphore_signal(barrier, inc=1, device_id=up, device_id_type=MESH)

    @pl.when(has_down)
    def _():
        pl.semaphore_signal(barrier, inc=1, device_id=down, device_id_type=MESH)
    pl.semaphore_wait(barrier, 4 + has_up.astype(jnp.int32) + has_down.astype(jnp.int32))

    mine = w.at[:, pl.ds(pl.multiple_of(y * half, 128), half)]
    deep = feat // CHUNKS

    def source(block, d, c):
        held = mine if d == 0 else wg.at[block]
        return held.at[c * deep:(c + 1) * deep]

    def up_copy(block, d, c):
        return remote(source(block, d, c), wg.at[block, c * deep:(c + 1) * deep], wu_s.at[d, c], wu_r.at[d, c], up)

    def down_copy(block, d, c):
        return remote(source(block, d, c), wg.at[block, c * deep:(c + 1) * deep], wd_s.at[d, c], wd_r.at[d, c], down)

    def start_own(c):
        @pl.when(has_up)
        def _():
            up_copy(z, 0, c).start()

        @pl.when((z < nz - 1) & has_down)
        def _():
            down_copy(z, 0, c).start()

    start_own(0)

    @pl.when(z == nz - 1)
    def _():
        for c in range(CHUNKS):
            down_copy(z, 0, c).start()
    own_w = pltpu.make_async_copy(mine, wg.at[z], own_sem.at[nz])
    own_w.start()

    def cot_piece(j, b):
        xj, yj = place(j)
        return cot.at[0, :, pl.ds(pl.multiple_of((b * 2 + xj) * wd + yj * half, 128), half)]

    def cot_own(b):
        return pltpu.make_async_copy(cot_piece(0, b), cotg.at[b, 0], own_sem.at[b])

    def cot_copy(j, b):
        return remote(cot_piece(j, b), cotg.at[b, j], c_s.at[j, b], c_r.at[j, b], to_peer(j))

    for b in range(nz):
        cot_own(b).start()
        for j in (1, 2, 3):
            cot_copy(j, b).start()

    def col(h):
        return slice(h * HS, (h + 1) * HS)

    def prefix_copy(g):
        part = pl.ds(g * per, per)
        return remote(pout.at[part], pin.at[part], p_s.at[g], p_r.at[g], up)

    def suffix_copy(g):
        part = pl.ds(g * per, per)
        return remote(sout.at[part], sin.at[part], x_s.at[g], x_r.at[g], down)

    for load in loads:
        load.wait()
    for g in range(CHUNKS):
        for h in range(g * per, (g + 1) * per):
            lst[h] = dot(k[0, :, col(h)], v[0, :, col(h)], 0, 0)

        @pl.when(z == 0)
        def _():
            part = slice(g * per, (g + 1) * per)
            pout[part] = lst[part].astype(BF16)
            pin[part] = jnp.zeros((per, HS, HS), BF16)
            prefix_copy(g).start()

    causal = (lax.broadcasted_iota(jnp.int32, (rows, rows), 1) <= lax.broadcasted_iota(jnp.int32, (rows, rows), 0))
    for h in range(head_count):
        product = dot(q[0, :, col(h)], k[0, :, col(h)], 1, 1)
        scores[h] = jnp.where(causal, product, 0.0).astype(BF16)
    for h in range(head_count):
        att[h] = dot(scores[h], v[0, :, col(h)], 1, 0)

    def normed_copy(j):
        return remote(normg.at[0], normg.at[j], n_s.at[j], n_r.at[j], to_peer(j))

    def grad_copy(j, c):
        part = slice(c * deep, (c + 1) * deep)
        return remote(ngs.at[j, :, part], ngr.at[j, :, part], g_s.at[j, c], g_r.at[j, c], to_peer(j))

    def attend():
        @pl.when(z > 0)
        def _():
            for g in range(CHUNKS):
                prefix_copy(g).wait_recv()

                @pl.when(has_up)
                def _():
                    part = slice(g * per, (g + 1) * per)
                    pout[part] = (pin[part].astype(F32) + lst[part]).astype(BF16)
                    prefix_copy(g).start()

        for h in range(head_count):
            total = att[h] + dot(q[0, :, col(h)], pin[h], 1, 0)
            att[h] = total
            factor = lax.rsqrt(jnp.mean(total * total, axis=-1, keepdims=True) + 1e-05)
            normg[0, :, col(h)] = (total * factor).astype(BF16)
        for j in (1, 2, 3):
            normed_copy(j).start()

    def turn(g):
        for j in (1, 2, 3):
            grad_copy(j, g).wait_recv()
        for h in range(g * per, (g + 1) * per):
            grad = acc[:, col(h)]
            for j in (1, 2, 3):
                grad = grad + ngr[j, :, col(h)].astype(F32)
            total = att[h]
            factor = lax.rsqrt(jnp.mean(total * total, axis=-1, keepdims=True) + 1e-05)
            mean_term = jnp.mean(total * grad, axis=-1, keepdims=True)
            turned = (factor * grad - total * (factor * factor * factor) * mean_term).astype(BF16)
            ag[h] = turned
            lst[h] = dot(q[0, :, col(h)], turned, 0, 0)

        @pl.when(z == nz - 1)
        def _():
            part = slice(g * per, (g + 1) * per)
            sout[part] = lst[part].astype(BF16)
            sin[part] = jnp.zeros((per, HS, HS), BF16)
            suffix_copy(g).start()

    for c in range(CHUNKS):
        if c + 1 < CHUNKS:
            start_own(c + 1)
        for d in range(1, nz):
            @pl.when(z - d >= 0)
            def _():
                up_copy(z - d, d - 1, c).wait_recv()

                @pl.when(has_up)
                def _():
                    up_copy(z - d, d, c).start()

            @pl.when(z + d < nz)
            def _():
                down_copy(z + d, d - 1, c).wait_recv()

                @pl.when(has_down)
                def _():
                    down_copy(z + d, d, c).start()
        if c == 0:
            own_w.wait()
            for b in range(nz):
                cot_own(b).wait()
                for j in (1, 2, 3):
                    cot_copy(j, b).wait_recv()
        part = slice(c * deep, (c + 1) * deep)
        total = dot(cotg[0].reshape(4 * rows, half), wg[0, part, :], 1, 1)
        for b in range(1, nz):
            total = total + dot(cotg[b].reshape(4 * rows, half), wg[b, part, :], 1, 1)
        acc[:, part] = total[:rows]
        for j in (1, 2, 3):
            ngs[j, :, part] = total[j * rows:(j + 1) * rows].astype(BF16)
            grad_copy(j, c).start()
        if c == 0:
            @pl.when(z <= 1)
            def _():
                attend()
        elif c < CHUNKS - 1:
            @pl.when(z == c + 1)
            def _():
                attend()
        if c == CHUNKS - 2:
            turn(0)
        if c == CHUNKS - 1:
            for g in range(1, CHUNKS - 1):
                turn(g)

    for j in (1, 2, 3):
        normed_copy(j).wait_recv()
    sub_copy = remote(osend, orecv, o_s.at[0], o_r.at[0], other)

    @pl.loop(0, hb)
    def _(i):
        left = normg[...].reshape(4 * rows, feat)
        osend[i] = dot(left, wg[(1 - s) * hb + i], 1, 0).astype(BF16).reshape(4, rows, half)
    sub_copy.start()

    @pl.loop(0, hb)
    def _(i):
        left = normg[...].reshape(4 * rows, feat)
        oacc[i] = dot(left, wg[s * hb + i], 1, 0).reshape(4, rows, half)

    turn(CHUNKS - 1)

    def out_copy(i, j):
        return remote(ofin.at[i, j], oin.at[i, j], f_s.at[i, j], f_r.at[i, j], to_peer(j))

    sub_copy.wait_recv()
    for i in range(hb):
        ofin[i] = (oacc[i] + orecv[i].astype(F32)).astype(BF16)
        for j in (1, 2, 3):
            out_copy(i, j).start()

    def hop():
        for g in range(CHUNKS):
            suffix_copy(g).wait_recv()

            @pl.when(has_down)
            def _():
                part = slice(g * per, (g + 1) * per)
                sout[part] = (sin[part].astype(F32) + lst[part]).astype(BF16)
                suffix_copy(g).start()

    @pl.when(z == nz - 2)
    def _():
        hop()

    for h in range(head_count):
        turned = ag[h]
        grad_scores = jnp.where(causal, dot(turned, v[0, :, col(h)], 1, 1), 0.0).astype(BF16)
        qg[0, :, col(h)] = (dot(turned, pin[h], 1, 1) + dot(grad_scores, k[0, :, col(h)], 1, 0)).astype(BF16)
        kloc[h] = dot(grad_scores, q[0, :, col(h)], 0, 0)
        vloc[h] = dot(scores[h], turned, 0, 0)

    @pl.when(z < nz - 2)
    def _():
        hop()

    for h in range(head_count):
        kg[0, :, col(h)] = (kloc[h] + dot(v[0, :, col(h)], sin[h], 1, 1)).astype(BF16)
        vg[0, :, col(h)] = (vloc[h] + dot(k[0, :, col(h)], sin[h], 1, 0)).astype(BF16)

    for i in range(hb):
        for j in range(4):
            xj, yj = place(j)
            part = pl.ds(pl.multiple_of((i * 2 + xj) * wd + yj * half, 128), half)
            if j == 0:
                out[0, :, part] = ofin[i, 0]
            else:
                out_copy(i, j).wait_recv()
                out[0, :, part] = oin[i, j]

    for c in range(CHUNKS):
        for d in range(nz - 1):
            @pl.when(has_up & (z - d >= 0))
            def _():
                up_copy(z, d, c).wait_send()

            @pl.when(has_down & (z + d < nz))
            def _():
                down_copy(z, d, c).wait_send()

    for g in range(CHUNKS):
        @pl.when(has_up)
        def _():
            prefix_copy(g).wait_send()

        @pl.when(has_down)
        def _():
            suffix_copy(g).wait_send()
    for j in (1, 2, 3):
        for b in range(nz):
            cot_copy(j, b).wait_send()
        normed_copy(j).wait_send()
        for c in range(CHUNKS):
            grad_copy(j, c).wait_send()
        for i in range(hb):
            out_copy(i, j).wait_send()
    sub_copy.wait_send()


def fused(nz, queries, key_vectors, value_vectors, out_weight, out_cotangent):
    rows, feat = queries.shape[1:]
    wd = out_weight.shape[1]
    heads, half, hb = feat // HS, wd // 2, nz // 2
    vmem, dma = pltpu.VMEM, pltpu.SemaphoreType.DMA
    states = (heads, HS, HS)
    inside = pl.BlockSpec(memory_space=pltpu.VMEM)
    outside = pl.BlockSpec(memory_space=pltpu.HBM)
    grads = jax.ShapeDtypeStruct((1, rows, feat), BF16)
    return tuple(pl.pallas_call(
        functools.partial(body, nz, heads, rows, wd),
        out_shape=(jax.ShapeDtypeStruct((1, rows, nz * wd), BF16), grads, grads, grads),
        in_specs=[outside] * 5,
        out_specs=(inside,) * 4,
        scratch_shapes=[
            vmem((nz, feat, half), BF16), vmem((nz, 4, rows, half), BF16),
            vmem(states, F32), vmem(states, BF16), vmem(states, BF16),
            vmem((heads, rows, rows), BF16), vmem((heads, rows, HS), F32),
            vmem((4, rows, feat), BF16), vmem((rows, feat), F32),
            vmem((4, rows, feat), BF16), vmem((4, rows, feat), BF16),
            vmem((hb, 4, rows, half), BF16), vmem((hb, 4, rows, half), BF16),
            vmem((hb, 4, rows, half), F32), vmem((hb, 4, rows, half), BF16), vmem((hb, 4, rows, half), BF16),
            vmem((heads, rows, HS), BF16), vmem((heads, rows, HS), F32), vmem((heads, rows, HS), F32),
            vmem(states, BF16), vmem(states, BF16),
            vmem((1, rows, feat), BF16), vmem((1, rows, feat), BF16), vmem((1, rows, feat), BF16), dma((3,)),
            dma((nz + 1,)), dma((nz, CHUNKS)), dma((nz, CHUNKS)), dma((nz, CHUNKS)), dma((nz, CHUNKS)),
            dma((4, nz)), dma((4, nz)), dma((CHUNKS,)), dma((CHUNKS,)), dma((CHUNKS,)), dma((CHUNKS,)),
            dma((4,)), dma((4,)), dma((4, CHUNKS)), dma((4, CHUNKS)), dma((1,)), dma((1,)), dma((hb, 4)), dma((hb, 4)),
        ],
        compiler_params=pltpu.CompilerParams(
            collective_id=0, has_side_effects=True, vmem_limit_bytes=60 * 1024 * 1024),
    )(queries, key_vectors, value_vectors, out_weight, out_cotangent))


def solution(mesh):
    placed = (
        P(("groups", "dp"), "seq", "sub"),
        P(("groups", "dp"), "seq", "sub"),
        P(("groups", "dp"), "seq", "sub"),
        P("sub", ("seq", "dp")),
        P(("groups", "dp"), "seq", None),
    )
    shape = dict(mesh.shape)
    count = shape["seq"]

    def part(queries, key_vectors, value_vectors, out_weight, out_cotangent):
        args = (queries, key_vectors, value_vectors, out_weight, out_cotangent)
        fits = shape["groups"] == shape["dp"] == shape["sub"] == 2 and count % 2 == 0
        if fits and count <= 4 and out_weight.shape[1] % 256 == 0:
            return fused(count, *args)
        return local(*args)

    return jax.shard_map(
        part,
        mesh=mesh,
        in_specs=placed,
        out_specs=(
            P(("groups", "dp"), "seq", "sub"),
            P(("groups", "dp"), "seq", "sub"),
            P(("groups", "dp"), "seq", "sub"),
            P(("groups", "dp"), "seq", "sub"),
        ),
        check_vma=False,
    )
```
